512 devices in a mesh: ctx: 32 (over x, y), ts: 16 (over z, core).
Axes of the slice: x: 4, y: 8, z: 8, core: 2. Of those that a mesh axis runs over, the one named last changes fastest.
Arguments:
- projected: bfloat16 [65536, 12288], P(('ctx', 'ts')), may hold values from -6 to 6
- doc_lengths: int32 [16], replicated, may hold values from 1 to 16384, 65536 in all
- short_taps: float32 [3, 7, 256], replicated, may hold values from -2.4 to 2.4
- medium_taps: float32 [128, 256], replicated, may hold values from -0.5 to 0.5
- decay_rates: float32 [16, 256], replicated, may hold values from 3.8146973e-06 to 0.03
- residues: float32 [16, 256], replicated, may hold values from -1.5 to 1.5
- skip_gain: float32 [4096], replicated, may hold values from -3 to 3
Outputs:
- hyena_out: bfloat16 [65536, 4096], P(('ctx', 'ts'))
The draws below stay inside these ranges and needn't reach their ends.
Inputs may be any that keep to these rules, and one draw needn't show every extreme that they name: `doc_lengths`: the lengths sum to 65536; the largest is exactly 16384.
All inputs are finite; a program needn't handle non-finite values.
Results may differ from the reference program's by a relative error of at most 0.01.
Values may be sent and summed in bfloat16 or wider, within the bound.
No kernel may reach another device: no remote copies, remote signals or barrier semaphores. Data moves between devices by JAX's collectives and lax.ppermute only.
A program may use at most 128 MiB of HBM per device.

```python
import math
import jax
import jax.numpy as jnp
import numpy as np
from jax import lax

D = 4096
GROUP = 16
SHORT = 7
MEDIUM = 128
MODES = 16
DOCS = 16
GROUPS = 256
LENGTH = 65536
MAXDOC = 16384


def levels(own_key, shape, shards, smallest, largest):
    def one(dim, shards_of):
        steps = jax.random.uniform(jax.random.fold_in(jax.random.fold_in(own_key, 6), dim), (shards_of,), jnp.float32, smallest / len(shards), largest / len(shards))
        return jnp.repeat(jnp.exp(steps), shape[dim] // shards_of).reshape((-1,) + (1,) * (len(shape) - dim - 1))

    loudness = one(*shards[0])
    for cut in shards[1:]:
        loudness = loudness * one(*cut)
    return loudness


def profile(amount, total, limit, slope):
    loads = [(1 << 20) // math.isqrt(grade ** slope) + 1 for grade in range(2, amount + 1)]
    rest, holding = total - limit - (amount - 1), [1] * (amount - 1)
    while rest > 0:
        free = [i for i in range(amount - 1) if holding[i] < limit]
        whole, budget = sum([loads[i] for i in free]), rest
        for i in free:
            extra = min(limit - holding[i], max(1, budget * loads[i] // whole), rest)
            holding[i] = holding[i] + extra
            rest = rest - extra
    return np.array([limit] + holding)


def uneven_parts(key, amount, total, reach, skew):
    if amount == 2:
        one = jax.random.randint(key, (), max(1, total - reach), min(reach, total - 1) + 1)
        return jnp.stack([one, total - one])
    lengths = jnp.asarray(profile(amount, total, reach, skew), jnp.int32)
    twos = (amount - 1) // 2
    source_of, taker = lengths[1:1 + 2 * twos:2], lengths[2:2 + 2 * twos:2]
    room = jnp.minimum(source_of - 1, reach - taker)
    moved = jax.random.randint(jax.random.fold_in(key, 1), (twos,), 0, 1 << 20) % (room + 1)
    lengths = lengths.at[1:1 + 2 * twos:2].set(source_of - moved).at[2:2 + 2 * twos:2].set(taker + moved)
    return lengths[jax.random.permutation(jax.random.fold_in(key, 2), amount)]


def normal_values(stream_key, shape, spread, limit, pieces=(), dtype=jnp.bfloat16):
    drawn = jax.random.normal(stream_key, shape, jnp.float32) * spread
    if len(pieces) > 0:
        drawn = levels(stream_key, shape, pieces, -0.22, 0.18) * drawn
    return jnp.clip(drawn, min=-limit, max=limit).astype(dtype)


def setup_inputs(seed: int = 0) -> dict:
    keys = jax.random.split(jax.random.key(seed), 8)
    return {
        "projected": normal_values(keys[0], (LENGTH, 3 * D), 1.0, 6.0, ((0, 512),)),
        "doc_lengths": uneven_parts(keys[1], DOCS, LENGTH, MAXDOC, 2).astype(jnp.int32),
        "short_taps": normal_values(keys[2], (3, SHORT, GROUPS), 0.4, 2.4, (), jnp.float32),
        "medium_taps": normal_values(keys[3], (MEDIUM, GROUPS), MEDIUM ** -0.5, 0.5, (), jnp.float32),
        "decay_rates": jnp.clip(jnp.exp(jax.random.uniform(keys[4], (MODES, GROUPS), jnp.float32, math.log(3.814697265625e-06), math.log(0.03))), 3.814697265625e-06, 0.03),
        "residues": normal_values(keys[5], (MODES, GROUPS), 0.25, 1.5, (), jnp.float32),
        "skip_gain": normal_values(keys[6], (D,), 0.5, 3.0, (), jnp.float32),
    }


HIGHEST = lax.Precision.HIGHEST

def starts_for(positions, doc_lengths):
    doc_ends = jnp.cumsum(doc_lengths).astype(jnp.int32)
    doc_begins = (doc_ends - doc_lengths).astype(jnp.int32)
    inside = doc_begins[None, :] <= positions[:, None]
    return lax.optimization_barrier(jnp.max(jnp.where(inside, doc_begins[None, :], 0), axis=1)).astype(jnp.int32)

def featurize(window, positions, row_start, tap_table):
    row_count = positions.shape[0]
    summed = jnp.zeros((row_count,) + window.shape[1:], jnp.float32)
    for offset in range(SHORT):
        in_doc = positions - offset >= row_start
        shifted = window[SHORT - 1 - offset:SHORT - 1 - offset + row_count]
        summed = summed + jnp.where(in_doc[:, None, None], shifted * tap_table[:, offset][None], 0.0)
    return summed

def filter_tables(decay_rates, residues):
    scaled = residues * jnp.sqrt(-jnp.expm1(-2.0 * decay_rates))
    steps_f = jnp.arange(MEDIUM).astype(jnp.float32)
    long_table = lax.optimization_barrier(jnp.sum(scaled[None] * jnp.exp(-decay_rates[None] * steps_f[:, None, None]), axis=1))
    return (scaled, long_table)

def band_matrix(medium_taps, long_table, row_pos, col_pos, block_begin):
    distance = row_pos[:, None] - col_pos[None, :]
    in_band = (distance >= 0) & (distance < MEDIUM)
    lag_index = jnp.clip(distance, 0, MEDIUM - 1)
    same_block = (col_pos >= block_begin)[None, :, None]
    tap_values = medium_taps[lag_index] + jnp.where(same_block, long_table[lag_index], 0.0)
    return jnp.where(in_band[:, :, None], tap_values, 0.0)

def reference(projected, doc_lengths, short_taps, medium_taps, decay_rates, residues, skip_gain):
    groups = D // GROUP
    scaled, long_table = filter_tables(decay_rates, residues)
    taps_full = jnp.repeat(short_taps, GROUP, axis=2)
    local_rows = jnp.arange(MEDIUM).astype(jnp.int32)
    local_f = local_rows.astype(jnp.float32)
    decay_rows = scaled[None] * jnp.exp(-decay_rates[None] * (local_f + 1.0)[:, None, None])
    tail_power = jnp.exp(-decay_rates[None] * (MEDIUM - 1.0 - local_f)[:, None, None])
    block_decay = jnp.exp(-decay_rates * MEDIUM)
    blocks_total = LENGTH // MEDIUM

    def advance(carry, block_idx):
        raw_prev, product_prev, modal_state = carry
        block_begin = (block_idx * MEDIUM).astype(jnp.int32)
        current = lax.dynamic_slice_in_dim(projected, block_begin, MEDIUM, 0).astype(jnp.float32).reshape(MEDIUM, 3, D)
        positions = block_begin + local_rows
        row_start = starts_for(positions, doc_lengths)
        window = jnp.concatenate([raw_prev, current], axis=0)
        feature = featurize(window, positions, row_start, taps_full)
        product = (feature[:, 1] * feature[:, 2]).astype(jnp.bfloat16)
        col_pos = block_begin - MEDIUM + jnp.arange(2 * MEDIUM).astype(jnp.int32)
        matrix = band_matrix(medium_taps, long_table, positions, col_pos, block_begin)
        allowed = col_pos[None, :] >= row_start[:, None]
        matrix = jnp.where(allowed[:, :, None], matrix, 0.0)
        window_x = jnp.concatenate([product_prev, product], axis=0).astype(jnp.float32).reshape(2 * MEDIUM, groups, GROUP)
        banded = jnp.einsum('tug,ugc->tgc', matrix, window_x, precision=HIGHEST).reshape(MEDIUM, D)
        carried_part = jnp.einsum('tmg,mgc->tgc', decay_rows, modal_state.reshape(MODES, groups, GROUP), precision=HIGHEST).reshape(MEDIUM, D)
        carried_part = jnp.where((row_start < block_begin)[:, None], carried_part, 0.0)
        product_f = product.astype(jnp.float32)
        filtered = (banded + carried_part + skip_gain[None, :] * product_f).astype(jnp.bfloat16)
        output = (feature[:, 0] * filtered.astype(jnp.float32)).astype(jnp.bfloat16)
        last_start = row_start[MEDIUM - 1]
        kept_rows = jnp.where((positions >= last_start)[:, None], product_f, 0.0).reshape(MEDIUM, groups, GROUP)
        contribution = jnp.einsum('umg,ugc->mgc', tail_power, kept_rows, precision=HIGHEST).reshape(MODES, D)
        factor = jnp.where(last_start < block_begin, block_decay, 0.0)
        modal_state = jnp.repeat(factor, GROUP, axis=1) * modal_state + contribution
        return ((window[MEDIUM:], product, modal_state), output)
    initial = (jnp.zeros((SHORT - 1, 3, D), jnp.float32), jnp.zeros((MEDIUM, D), jnp.bfloat16), jnp.zeros((MODES, D), jnp.float32))
    finals, outputs = lax.scan(advance, initial, jnp.arange(blocks_total).astype(jnp.int32))
    return outputs.reshape(LENGTH, D)
```

```python
import jax
import jax.numpy as jnp
from jax import lax
from jax.experimental import pallas as pl
from jax.experimental.pallas import tpu as pltpu
from jax.sharding import PartitionSpec as P

GROUP = 16
SHORT = 7
BLOCK = 128
MODES = 16
LANES = 128
DOCS = 16
SPAN = 4
PER_TILE = LANES // GROUP
FLAT = ("ctx", "ts")
HIGHEST = lax.Precision.HIGHEST
f32 = jnp.float32
bf16 = jnp.bfloat16
i32 = jnp.int32


def iota(shape, dim):
    return lax.broadcasted_iota(i32, shape, dim)


def tile_at(i):
    return pl.ds(pl.multiple_of(i * LANES, LANES), LANES)


def in_vmem():
    return pl.BlockSpec(memory_space=pltpu.VMEM)


def in_smem():
    return pl.BlockSpec(memory_space=pltpu.SMEM)


def params():
    return pltpu.CompilerParams(vmem_limit_bytes=48 << 20)


def dot_nt(a, b, precision=None):
    return lax.dot_general(
        a, b, (((1,), (1,)), ((), ())), precision=precision, preferred_element_type=f32
    )


def tables_kernel(
    base_ref, docs_ref, taps_ref, rates_ref, scaled_ref, medium_ref,
    srel_ref, live_ref, tapsx_ref, ratesx_ref, dec_ref, tail_ref, own_ref, med_ref,
    stack_ref,
):
    base = base_ref[0]
    first = base_ref[1]
    row = iota((BLOCK, LANES), 0)
    lane = iota((BLOCK, LANES), 1)
    pos = base + row
    starts = jnp.zeros((BLOCK, LANES), i32)
    ends = first + row * BLOCK + (BLOCK - 1)
    lasts = jnp.zeros((BLOCK, LANES), i32)
    begin = jnp.int32(0)
    for d in range(DOCS):
        starts = jnp.where(pos >= begin, begin, starts)
        lasts = jnp.where(ends >= begin, begin, lasts)
        begin = begin + docs_ref[d]
    srel_ref[...] = starts - base
    live = jnp.where(lasts < ends - (BLOCK - 1), 1.0, 0.0)
    live_ref[...] = live[: live_ref.shape[0]]
    stack_ref[...] = jnp.zeros(stack_ref.shape, f32)
    for p in range(3):
        stack_ref[8 * p : 8 * p + SHORT] = taps_ref[p]
    stack_ref[24:40] = rates_ref[...]
    stack_ref[40:56] = scaled_ref[...]
    whole = stack_ref[...]
    upper = whole.astype(bf16)
    rest = whole - upper.astype(f32)
    middle = rest.astype(bf16)
    lower = (rest - middle.astype(f32)).astype(bf16)
    pieces = jnp.concatenate([upper, middle, lower], axis=0)
    flip = jnp.where(row + lane == BLOCK - 1, 1.0, 0.0)
    med_ref[...] = jnp.dot(
        medium_ref[...].T, flip, precision=HIGHEST, preferred_element_type=f32
    )
    old = starts < base
    groups = medium_ref.shape[1]
    g_row = iota((groups, LANES), 0)
    g_lane = iota((groups, LANES), 1) // GROUP
    own_mode = iota((MODES, LANES), 0) == iota((MODES, LANES), 1) % MODES
    own_group = iota((PER_TILE, LANES), 0) == iota((PER_TILE, LANES), 1) // MODES
    ahead = (row + 1).astype(f32)
    behind = (BLOCK - 1 - row).astype(f32)

    def step(i, carry):
        hot = jnp.where(g_lane + i * PER_TILE == g_row, 1.0, 0.0).astype(bf16)
        spread = jnp.dot(pieces, hot, preferred_element_type=f32)
        spread = spread[0:56] + spread[56:112] + spread[112:168]
        tapsx_ref[:, tile_at(i)] = spread[0:24]
        ratesx_ref[:, tile_at(i)] = spread[24:40]
        rate = jnp.sum(jnp.where(own_mode, spread[24:40], 0.0), axis=0, keepdims=True)
        scale = jnp.sum(jnp.where(own_mode, spread[40:56], 0.0), axis=0, keepdims=True)
        decay = jnp.where(old, scale * jnp.exp(-rate * ahead), 0.0)
        dec_ref[:, tile_at(i)] = decay.astype(bf16)
        power = jnp.exp(-rate * behind)
        tail_ref[tile_at(i), :] = power.T.astype(bf16)
        picked = jnp.where(own_group, scale, 0.0)
        rows = pl.ds(pl.multiple_of(i * PER_TILE, PER_TILE), PER_TILE)
        own_ref[rows, :] = med_ref[rows, :] + dot_nt(picked, power, HIGHEST)
        return carry

    lax.fori_loop(0, tapsx_ref.shape[1] // LANES, step, 0)


def make_tables(place, doc_lengths, short_taps, medium_taps, decay_rates, scaled, width):
    groups = medium_taps.shape[1]
    shape = jax.ShapeDtypeStruct
    return pl.pallas_call(
        tables_kernel,
        out_shape=(
            shape((BLOCK, LANES), i32),
            shape((4 * DOCS, LANES), f32),
            shape((24, width), f32),
            shape((MODES, width), f32),
            shape((BLOCK, width), bf16),
            shape((width, BLOCK), bf16),
            shape((groups, BLOCK), f32),
            shape((groups, BLOCK), f32),
        ),
        in_specs=[in_smem(), in_smem()] + [in_vmem()] * 4,
        out_specs=tuple([in_vmem()] * 8),
        scratch_shapes=[pltpu.VMEM((56, groups), f32)],
        compiler_params=params(),
        name="tables",
    )(place, doc_lengths, short_taps, decay_rates, scaled, medium_taps)


def feature_of(raw_ref, halo_ref, taps_ref, part, i, rel, window_ref):
    window_ref[0:8] = halo_ref[:, tile_at(i)].astype(f32)
    window_ref[8 : 8 + BLOCK] = raw_ref[:, tile_at(i)].astype(f32)
    summed = jnp.zeros((BLOCK, LANES), f32)
    for offset in range(SHORT):
        tap = taps_ref[8 * part + offset : 8 * part + offset + 1, tile_at(i)]
        term = window_ref[8 - offset : 8 - offset + BLOCK] * tap
        if offset:
            term = jnp.where(rel >= offset, term, 0.0)
        summed = summed + term
    return summed


def product_kernel(
    k_ref, v_ref, hk_ref, hv_ref, taps_ref, srel_ref, tail_ref,
    product_ref, contrib_ref,
    wk_ref, wv_ref,
):
    row = iota((BLOCK, LANES), 0)
    rel = row - srel_ref[...]
    kept = jnp.where(row >= srel_ref[BLOCK - 1 : BLOCK], 1.0, 0.0).astype(bf16)
    lane_group = iota((MODES, LANES), 1) // GROUP

    def step(i, carry):
        key = feature_of(k_ref, hk_ref, taps_ref, 1, i, rel, wk_ref)
        value = feature_of(v_ref, hv_ref, taps_ref, 2, i, rel, wv_ref)
        product = (key * value).astype(bf16)
        product_ref[:, tile_at(i)] = product
        all_modes = jnp.dot(
            tail_ref[tile_at(i), :], product * kept, preferred_element_type=f32
        )
        contrib = all_modes[0:MODES]
        for g in range(1, PER_TILE):
            contrib = jnp.where(
                lane_group == g, all_modes[g * MODES : (g + 1) * MODES], contrib
            )
        contrib_ref[0, i] = contrib[0:8].astype(bf16)
        contrib_ref[1, i] = contrib[8:16].astype(bf16)
        return carry

    lax.fori_loop(0, product_ref.shape[1] // LANES, step, 0)


def make_product(projected, halo, tapsx, srel, tail):
    width = projected.shape[1] // 3
    shape = jax.ShapeDtypeStruct
    return pl.pallas_call(
        product_kernel,
        grid=(1,),
        out_shape=(
            shape((BLOCK, width), bf16),
            shape((2, width // LANES, 8, LANES), bf16),
        ),
        in_specs=[
            pl.BlockSpec((BLOCK, width), lambda _: (0, 1)),
            pl.BlockSpec((BLOCK, width), lambda _: (0, 2)),
            pl.BlockSpec((8, width), lambda _: (0, 1)),
            pl.BlockSpec((8, width), lambda _: (0, 2)),
            in_vmem(),
            in_vmem(),
            in_vmem(),
        ],
        out_specs=(in_vmem(), in_vmem()),
        scratch_shapes=[pltpu.VMEM((8 + BLOCK, LANES), f32)] * 2,
        compiler_params=params(),
        name="product",
    )(projected, projected, halo, halo, tapsx, srel, tail)


def band_sum(i, x_ref, taps_ref, mask, acc):
    lane_group = iota((1, LANES), 1) // GROUP
    even = jnp.where(lane_group % 2 == 0, 1.0, 0.0).astype(bf16)
    odd = jnp.where(lane_group % 2 == 1, 1.0, 0.0).astype(bf16)
    x = x_ref[:, tile_at(i)]
    both = jnp.concatenate([x * even, x * odd], axis=0)
    pair_of = iota((BLOCK, LANES), 1) // (2 * GROUP)
    taps = taps_ref[pl.ds(pl.multiple_of(i * PER_TILE, PER_TILE), PER_TILE), :]
    for pair in range(PER_TILE // 2):
        bands = []
        for side in range(2):
            g = 2 * pair + side
            line = jnp.broadcast_to(taps[g : g + 1], (BLOCK, BLOCK))
            ring = pltpu.roll(line, 1, 1, stride=1, stride_axis=0)
            bands.append((ring * mask).astype(bf16))
        out = jnp.dot(
            jnp.concatenate(bands, axis=1), both, preferred_element_type=f32
        )
        acc = jnp.where(pair_of == pair, acc + out, acc)
    return acc


def own_kernel(
    q_ref, hq_ref, taps_ref, srel_ref, x_ref, own_ref, skip_ref,
    query_ref, acc_ref,
    wq_ref, mask_ref,
):
    row = iota((BLOCK, LANES), 0)
    lane = iota((BLOCK, LANES), 1)
    rel = row - srel_ref[...]
    mask_ref[...] = jnp.where((lane <= row) & (lane >= srel_ref[...]), 1.0, 0.0)

    def step(i, carry):
        query_ref[:, tile_at(i)] = feature_of(q_ref, hq_ref, taps_ref, 0, i, rel, wq_ref)
        acc = skip_ref[:, tile_at(i)] * x_ref[:, tile_at(i)].astype(f32)
        acc_ref[:, tile_at(i)] = band_sum(i, x_ref, own_ref, mask_ref[...], acc)
        return carry

    lax.fori_loop(0, acc_ref.shape[1] // LANES, step, 0)


def make_own(projected, halo, tapsx, srel, product, own, skip):
    width = product.shape[1]
    shape = jax.ShapeDtypeStruct
    return pl.pallas_call(
        own_kernel,
        grid=(1,),
        out_shape=(shape((BLOCK, width), f32), shape((BLOCK, width), f32)),
        in_specs=[
            pl.BlockSpec((BLOCK, width), lambda _: (0, 0)),
            pl.BlockSpec((8, width), lambda _: (0, 0)),
        ]
        + [in_vmem()] * 5,
        out_specs=(in_vmem(), in_vmem()),
        scratch_shapes=[
            pltpu.VMEM((8 + BLOCK, LANES), f32),
            pltpu.VMEM((BLOCK, LANES), f32),
        ],
        compiler_params=params(),
        name="own",
    )(projected, halo, tapsx, srel, product, own, skip)


def earlier_kernel(x_ref, taps_ref, srel_ref, acc_ref, out_ref, mask_ref):
    row = iota((BLOCK, LANES), 0)
    lane = iota((BLOCK, LANES), 1)
    inside = (lane > row) & (lane - BLOCK >= srel_ref[...])
    mask_ref[...] = jnp.where(inside, 1.0, 0.0)

    def step(i, carry):
        acc = acc_ref[:, tile_at(i)]
        out_ref[:, tile_at(i)] = band_sum(i, x_ref, taps_ref, mask_ref[...], acc)
        return carry

    lax.fori_loop(0, out_ref.shape[1] // LANES, step, 0)


def make_earlier(before, med, srel, acc):
    return pl.pallas_call(
        earlier_kernel,
        out_shape=jax.ShapeDtypeStruct(acc.shape, f32),
        in_specs=[in_vmem()] * 4,
        out_specs=in_vmem(),
        scratch_shapes=[pltpu.VMEM((BLOCK, LANES), f32)],
        compiler_params=params(),
        name="earlier",
    )(before, med, srel, acc)


def totals_kernel(which_ref, terms_ref, rates_ref, live_ref, out_ref):
    decay = jnp.exp(-rates_ref[...] * float(BLOCK))
    state = jnp.zeros((8, LANES), f32)
    kept = jnp.ones((8, LANES), f32)
    for b in range(terms_ref.shape[0]):
        factor = live_ref[b : b + 1] * decay
        state = factor * state + terms_ref[b].astype(f32)
        kept = factor * kept
    out_ref[0] = state
    out_ref[1] = kept


def item_spec(tiles):
    return pl.BlockSpec((8, LANES), lambda _, which: (which[0] // tiles, which[0] % tiles))


def make_totals(which, terms, ratesx, live):
    tiles = ratesx.shape[1] // LANES
    return pl.pallas_call(
        totals_kernel,
        out_shape=jax.ShapeDtypeStruct((2, 8, LANES), f32),
        grid_spec=pltpu.PrefetchScalarGridSpec(
            num_scalar_prefetch=1,
            grid=(1,),
            in_specs=[in_vmem(), item_spec(tiles), in_vmem()],
            out_specs=in_vmem(),
        ),
        compiler_params=params(),
        name="totals",
    )(which, terms, ratesx, live)


def states_kernel(which_ref, terms_ref, rates_ref, live_ref, one_ref, two_ref, out_ref):
    decay = jnp.exp(-rates_ref[...] * float(BLOCK))
    state = one_ref[0] + one_ref[1] * two_ref[...]
    for b in range(terms_ref.shape[0]):
        out_ref[b] = state.astype(bf16)
        state = live_ref[b : b + 1] * decay * state + terms_ref[b].astype(f32)


def make_states(which, terms, ratesx, live, one, two):
    tiles = ratesx.shape[1] // LANES
    return pl.pallas_call(
        states_kernel,
        out_shape=jax.ShapeDtypeStruct(terms.shape, bf16),
        grid_spec=pltpu.PrefetchScalarGridSpec(
            num_scalar_prefetch=1,
            grid=(1,),
            in_specs=[in_vmem(), item_spec(tiles)] + [in_vmem()] * 3,
            out_specs=in_vmem(),
        ),
        compiler_params=params(),
        name="states",
    )(which, terms, ratesx, live, one, two)


def final_kernel(acc_ref, query_ref, dec_ref, state_ref, out_ref):
    same = iota((LANES, LANES), 0) // MODES == iota((LANES, LANES), 1) // GROUP
    keep = jnp.where(same, 1.0, 0.0).astype(bf16)

    def step(i, carry):
        one = jnp.concatenate([state_ref[0, i], state_ref[1, i]], axis=0)
        spread = jnp.concatenate([one] * PER_TILE, axis=0) * keep
        carried = jnp.dot(dec_ref[:, tile_at(i)], spread, preferred_element_type=f32)
        filtered = (acc_ref[:, tile_at(i)] + carried).astype(bf16).astype(f32)
        out_ref[:, tile_at(i)] = (query_ref[:, tile_at(i)] * filtered).astype(bf16)
        return carry

    lax.fori_loop(0, out_ref.shape[1] // LANES, step, 0)


def make_final(acc, query, dec, state):
    return pl.pallas_call(
        final_kernel,
        out_shape=jax.ShapeDtypeStruct(acc.shape, bf16),
        in_specs=[in_vmem()] * 4,
        out_specs=in_vmem(),
        compiler_params=params(),
        name="final",
    )(acc, query, dec, state)


def per_device(projected, doc_lengths, short_taps, medium_taps, decay_rates, residues, skip_gain):
    ts_count = lax.axis_size("ts")
    ctx_count = lax.axis_size("ctx")
    count = ts_count * ctx_count
    ctx = lax.axis_index("ctx")
    index = ctx * ts_count + lax.axis_index("ts")
    size = SPAN * ts_count
    which = (index % size).astype(i32)
    groups = [[s * size + j for j in range(size)] for s in range(count // size)]
    onward = [(i, i + 1) for i in range(count - 1)]
    width = projected.shape[1] // 3

    def from_ctx(value, by):
        return lax.ppermute(value, "ctx", [(i, i + by) for i in range(ctx_count - by)])

    halo = lax.ppermute(projected[BLOCK - 8 :], FLAT, onward)
    place = jnp.stack([index * BLOCK, (index - which) * BLOCK]).astype(i32)
    scaled = residues * jnp.sqrt(-jnp.expm1(-2.0 * decay_rates))
    srel, live, tapsx, ratesx, dec, tail, own, med = make_tables(
        place, doc_lengths, short_taps, medium_taps, decay_rates, scaled, width
    )
    product, contrib = make_product(projected, halo, tapsx, srel, tail)
    items = contrib.reshape(size, 8, LANES)
    terms = lax.all_to_all(
        items, FLAT, split_axis=0, concat_axis=0, tiled=True, axis_index_groups=groups
    )
    before = lax.ppermute(product, FLAT, onward)
    query, acc = make_own(projected, halo, tapsx, srel, product, own, skip_gain.reshape(1, -1))
    ours = which.reshape(1)
    totals = make_totals(ours, terms, ratesx, live)
    one = from_ctx(totals, SPAN)
    two = from_ctx(totals[0], 2 * SPAN)
    states = make_states(ours, terms, ratesx, live, one, two)
    back = lax.all_to_all(
        states, FLAT, split_axis=0, concat_axis=0, tiled=True, axis_index_groups=groups
    )
    acc = make_earlier(before, med, srel, acc)
    return make_final(acc, query, dec, back.reshape(2, width // LANES, 8, LANES))


def solution(mesh):
    return jax.shard_map(
        per_device,
        mesh=mesh,
        in_specs=(P(FLAT, None), P(), P(), P(), P(), P(), P()),
        out_specs=P(FLAT, None),
        check_vma=False,
    )
```

```python
import jax
import jax.numpy as jnp
from jax import lax
from jax.experimental import pallas as pl
from jax.experimental.pallas import tpu as pltpu
from jax.sharding import PartitionSpec as P

GROUP = 16
SHORT = 7
BLOCK = 128
MODES = 16
LANES = 128
DOCS = 16
SPAN = 4
PER_TILE = LANES // GROUP
FLAT = ("ctx", "ts")
HIGHEST = lax.Precision.HIGHEST
f32 = jnp.float32
bf16 = jnp.bfloat16
i32 = jnp.int32


def iota(shape, dim):
    return lax.broadcasted_iota(i32, shape, dim)


TILES = 4
WIDE = TILES * LANES


def tile(j):
    return slice(j * LANES, (j + 1) * LANES)


def in_vmem():
    return pl.BlockSpec(memory_space=pltpu.VMEM)


def in_smem():
    return pl.BlockSpec(memory_space=pltpu.SMEM)


def columns(rows, first=0):
    return pl.BlockSpec((rows, WIDE), lambda j: (0, first + j))


def rows_of(count):
    return pl.BlockSpec((count, LANES), lambda j: (j, 0))


def fixed(shape):
    return pl.BlockSpec(shape, lambda j: (0,) * len(shape))


def hbm(*values):
    return [pltpu.with_memory_space_constraint(value, pltpu.HBM) for value in values]


def params(mib=12):
    return pltpu.CompilerParams(vmem_limit_bytes=mib << 20)


def spread_kernel(
    place_ref, stack_ref,
    srel_ref, live_ref, tapsx_ref, ratesx_ref, scalex_ref, tail_ref,
    pieces_ref,
):
    step = pl.program_id(0)
    row = iota((BLOCK, LANES), 0)

    @pl.when(step == 0)
    def _():
        base = place_ref[0]
        pos = base + row
        starts = jnp.zeros((BLOCK, LANES), i32)
        ends = place_ref[1] + row[: live_ref.shape[0]] * BLOCK + (BLOCK - 1)
        lasts = jnp.zeros(live_ref.shape, i32)
        begin = jnp.int32(0)
        for d in range(DOCS):
            starts = jnp.where(pos >= begin, begin, starts)
            lasts = jnp.where(ends >= begin, begin, lasts)
            begin = begin + place_ref[2 + d]
        srel_ref[...] = starts - base
        live_ref[...] = jnp.where(lasts < ends - (BLOCK - 1), 1.0, 0.0)
        whole = stack_ref[...]
        upper = whole.astype(bf16)
        rest = whole - upper.astype(f32)
        middle = rest.astype(bf16)
        pieces_ref[0] = upper
        pieces_ref[1] = middle
        pieces_ref[2] = (rest - middle.astype(f32)).astype(bf16)

    groups = stack_ref.shape[1]
    pieces = jnp.concatenate([pieces_ref[0], pieces_ref[1], pieces_ref[2]], axis=0)
    ahead = iota((groups, LANES), 0) - iota((groups, LANES), 1) // GROUP
    own_mode = iota((MODES, LANES), 0) == iota((MODES, LANES), 1) % MODES
    behind = (BLOCK - 1 - row).astype(f32)
    for j in range(TILES):
        first = (step * TILES + j) * PER_TILE
        hot = jnp.where(ahead == first, 1.0, 0.0).astype(bf16)
        spread = jnp.dot(pieces, hot, preferred_element_type=f32)
        spread = spread[0:64] + spread[64:128] + spread[128:192]
        tapsx_ref[:, tile(j)] = spread[0:24]
        ratesx_ref[:, tile(j)] = spread[24:40]
        scalex_ref[:, tile(j)] = spread[40:56]
        rate = jnp.sum(jnp.where(own_mode, spread[24:40], 0.0), axis=0, keepdims=True)
        tail_ref[tile(j), :] = jnp.exp(-rate * behind).T.astype(bf16)


def make_spread(place, stack, width):
    shape = pltpu.HBM
    return pl.pallas_call(
        spread_kernel,
        grid=(width // WIDE,),
        out_shape=(
            shape((BLOCK, LANES), i32),
            shape((4 * DOCS, LANES), f32),
            shape((24, width), f32),
            shape((MODES, width), f32),
            shape((MODES, width), f32),
            shape((width, BLOCK), bf16),
        ),
        in_specs=[in_smem(), fixed(stack.shape)],
        out_specs=(
            fixed((BLOCK, LANES)),
            fixed((4 * DOCS, LANES)),
            columns(24),
            columns(MODES),
            columns(MODES),
            rows_of(WIDE),
        ),
        scratch_shapes=[pltpu.VMEM((3, *stack.shape), bf16)],
        compiler_params=params(),
        name="spread",
    )(place, stack)


def tables_kernel(
    srel_ref, ratesx_ref, scalex_ref, medium_ref,
    dec_ref, own_ref, med_ref,
    long_ref,
):
    step = pl.program_id(0)
    row = iota((BLOCK, LANES), 0)
    lane = iota((BLOCK, LANES), 1)
    old = srel_ref[...] < 0
    own_mode = iota((MODES, LANES), 0) == iota((MODES, LANES), 1) % MODES
    ahead = (row + 1).astype(f32)
    behind = (BLOCK - 1 - row).astype(f32)
    steps_each = LANES // (TILES * PER_TILE)

    @pl.when(step % steps_each == 0)
    def _():
        long_ref[step // steps_each] = jnp.zeros((BLOCK, LANES), f32)

    total = long_ref[step // steps_each]
    for j in range(TILES):
        rate = jnp.sum(jnp.where(own_mode, ratesx_ref[:, tile(j)], 0.0), axis=0, keepdims=True)
        scale = jnp.sum(jnp.where(own_mode, scalex_ref[:, tile(j)], 0.0), axis=0, keepdims=True)
        decay = jnp.where(old, scale * jnp.exp(-rate * ahead), 0.0)
        dec_ref[:, tile(j)] = decay.astype(bf16)
        power = scale * jnp.exp(-rate * behind)
        upper = power.astype(bf16)
        lower = (power - upper.astype(f32)).astype(bf16)
        first = (step % steps_each * TILES + j) * PER_TILE
        hot = jnp.where(lane - row // MODES == first, 1.0, 0.0).astype(bf16)
        total = total + jnp.dot(
            jnp.concatenate([upper, lower], axis=1),
            jnp.concatenate([hot, hot], axis=0),
            preferred_element_type=f32,
        )
    long_ref[step // steps_each] = total

    @pl.when(step == pl.num_programs(0) - 1)
    def _():
        flip = jnp.where(row + lane == BLOCK - 1, 1.0, 0.0)
        for h in range(long_ref.shape[0]):
            medium = jnp.dot(
                flip, medium_ref[:, tile(h)], precision=HIGHEST, preferred_element_type=f32
            )
            med_ref[tile(h), :] = medium.T
            own_ref[tile(h), :] = (medium + long_ref[h]).T


def make_tables(srel, ratesx, scalex, medium_taps):
    width = ratesx.shape[1]
    groups = medium_taps.shape[1]
    shape = pltpu.HBM
    return pl.pallas_call(
        tables_kernel,
        grid=(width // WIDE,),
        out_shape=(
            shape((BLOCK, width), bf16),
            shape((groups, BLOCK), f32),
            shape((groups, BLOCK), f32),
        ),
        in_specs=[
            fixed((BLOCK, LANES)),
            columns(MODES),
            columns(MODES),
            fixed(medium_taps.shape),
        ],
        out_specs=(columns(BLOCK), fixed((groups, BLOCK)), fixed((groups, BLOCK))),
        scratch_shapes=[pltpu.VMEM((groups // LANES, BLOCK, LANES), f32)],
        compiler_params=params(),
        name="tables",
    )(*hbm(srel, ratesx, scalex, medium_taps))


def feature_of(raw_ref, halo_ref, taps_ref, part, j, rel, window_ref):
    window_ref[0:8] = halo_ref[:, tile(j)].astype(f32)
    window_ref[8 : 8 + BLOCK] = raw_ref[:, tile(j)].astype(f32)
    summed = window_ref[8 : 8 + BLOCK] * taps_ref[8 * part : 8 * part + 1, tile(j)]
    for offset in range(1, SHORT):
        tap = taps_ref[8 * part + offset : 8 * part + offset + 1, tile(j)]
        term = window_ref[8 - offset : 8 - offset + BLOCK] * tap
        summed = summed + jnp.where(rel >= offset, term, 0.0)
    return summed


def product_kernel(
    k_ref, v_ref, hq_ref, hk_ref, hv_ref, taps_ref, srel_ref, tail_ref,
    product_ref, contrib_ref, edge_ref,
    wk_ref, wv_ref,
):
    row = iota((BLOCK, LANES), 0)
    rel = row - srel_ref[...]
    kept = jnp.where(row >= srel_ref[BLOCK - 1 : BLOCK], 1.0, 0.0).astype(bf16)
    lane_group = iota((MODES, LANES), 1) // GROUP
    edge_ref[...] = hq_ref[...]
    for j in range(TILES):
        key = feature_of(k_ref, hk_ref, taps_ref, 1, j, rel, wk_ref.at[j])
        value = feature_of(v_ref, hv_ref, taps_ref, 2, j, rel, wv_ref.at[j])
        product = (key * value).astype(bf16)
        product_ref[:, tile(j)] = product
        all_modes = jnp.dot(
            tail_ref[tile(j), :], product * kept, preferred_element_type=f32
        )
        contrib = all_modes[0:MODES]
        for g in range(1, PER_TILE):
            contrib = jnp.where(
                lane_group == g, all_modes[g * MODES : (g + 1) * MODES], contrib
            )
        contrib_ref[0, j] = contrib[0:8].astype(bf16)
        contrib_ref[1, j] = contrib[8:16].astype(bf16)


def make_product(projected, halo, tapsx, srel, tail):
    width = projected.shape[1] // 3
    steps = width // WIDE
    shape = pltpu.HBM
    return pl.pallas_call(
        product_kernel,
        grid=(steps,),
        out_shape=(
            shape((BLOCK, width), bf16),
            shape((2, width // LANES, 8, LANES), bf16),
            shape((8, width), bf16),
        ),
        in_specs=[
            columns(BLOCK, steps),
            columns(BLOCK, 2 * steps),
            columns(8),
            columns(8, steps),
            columns(8, 2 * steps),
            columns(24),
            fixed((BLOCK, LANES)),
            rows_of(WIDE),
        ],
        out_specs=(
            columns(BLOCK),
            pl.BlockSpec((2, TILES, 8, LANES), lambda j: (0, j, 0, 0)),
            columns(8),
        ),
        scratch_shapes=[pltpu.VMEM((TILES, 8 + BLOCK, LANES), f32)] * 2,
        compiler_params=params(),
        name="product",
    )(*hbm(projected, projected), halo, halo, halo, *hbm(tapsx, srel, tail))


def band_sum(j, x_ref, taps_ref, mask_ref, acc):
    lane_group = iota((1, LANES), 1) // GROUP
    even = jnp.where(lane_group % 2 == 0, 1.0, 0.0).astype(bf16)
    odd = jnp.where(lane_group % 2 == 1, 1.0, 0.0).astype(bf16)
    x = x_ref[:, tile(j)]
    both = jnp.concatenate([x * even, x * odd], axis=0)
    pair_of = iota((BLOCK, LANES), 1) // (2 * GROUP)
    pairs = []
    for pair in range(PER_TILE // 2):
        bands = []
        for side in range(2):
            g = j * PER_TILE + 2 * pair + side
            line = jnp.broadcast_to(taps_ref[g : g + 1], (8, BLOCK))
            ring = pltpu.roll(line, 1, 1, stride=1, stride_axis=0)
            parts = [ring] + [pltpu.roll(ring, 8 * k, 1) for k in range(1, BLOCK // 8)]
            bands.append((jnp.concatenate(parts, axis=0) * mask_ref[...]).astype(bf16))
        pairs.append(jnp.concatenate(bands, axis=1))
    out = jnp.dot(jnp.concatenate(pairs, axis=0), both, preferred_element_type=f32)
    picked = out[0:BLOCK]
    for pair in range(1, PER_TILE // 2):
        picked = jnp.where(pair_of == pair, out[pair * BLOCK : (pair + 1) * BLOCK], picked)
    return acc + picked


def own_kernel(
    q_ref, hq_ref, taps_ref, srel_ref, x_ref, own_ref, skip_ref,
    query_ref, acc_ref, zero_ref,
    wq_ref, mask_ref,
):
    row = iota((BLOCK, LANES), 0)
    lane = iota((BLOCK, LANES), 1)
    rel = row - srel_ref[...]
    zero_ref[...] = jnp.zeros(zero_ref.shape, f32)

    @pl.when(pl.program_id(0) == 0)
    def _():
        mask_ref[...] = jnp.where((lane <= row) & (lane >= srel_ref[...]), 1.0, 0.0)

    for j in range(TILES):
        query_ref[:, tile(j)] = feature_of(q_ref, hq_ref, taps_ref, 0, j, rel, wq_ref.at[j])
        acc = skip_ref[:, tile(j)] * x_ref[:, tile(j)].astype(f32)
        acc_ref[:, tile(j)] = band_sum(j, x_ref, own_ref, mask_ref, acc)


def make_own(projected, halo, tapsx, srel, product, own, skip):
    width = product.shape[1]
    shape = pltpu.HBM
    return pl.pallas_call(
        own_kernel,
        grid=(width // WIDE,),
        out_shape=(
            shape((BLOCK, width), f32),
            shape((BLOCK, width), f32),
            shape((8, LANES), f32),
        ),
        in_specs=[
            columns(BLOCK),
            columns(8),
            columns(24),
            fixed((BLOCK, LANES)),
            columns(BLOCK),
            rows_of(WIDE // GROUP),
            columns(1),
        ],
        out_specs=(columns(BLOCK), columns(BLOCK), fixed((8, LANES))),
        scratch_shapes=[
            pltpu.VMEM((TILES, 8 + BLOCK, LANES), f32),
            pltpu.VMEM((BLOCK, LANES), f32),
        ],
        compiler_params=params(),
        name="own",
    )(*hbm(projected, halo, tapsx, srel, product, own, skip))


def earlier_kernel(x_ref, taps_ref, srel_ref, acc_ref, out_ref, mask_ref):
    row = iota((BLOCK, LANES), 0)
    lane = iota((BLOCK, LANES), 1)

    @pl.when(pl.program_id(0) == 0)
    def _():
        inside = (lane > row) & (lane - BLOCK >= srel_ref[...])
        mask_ref[...] = jnp.where(inside, 1.0, 0.0)

    for j in range(TILES):
        out_ref[:, tile(j)] = band_sum(j, x_ref, taps_ref, mask_ref, acc_ref[:, tile(j)])


def make_earlier(before, med, srel, acc):
    return pl.pallas_call(
        earlier_kernel,
        grid=(acc.shape[1] // WIDE,),
        out_shape=pltpu.HBM(acc.shape, f32),
        in_specs=[
            columns(BLOCK),
            rows_of(WIDE // GROUP),
            fixed((BLOCK, LANES)),
            columns(BLOCK),
        ],
        out_specs=columns(BLOCK),
        scratch_shapes=[pltpu.VMEM((BLOCK, LANES), f32)],
        compiler_params=params(),
        name="earlier",
    )(before, *hbm(med, srel, acc))


def totals_kernel(which_ref, terms_ref, rates_ref, live_ref, zero_ref, out_ref):
    decay = jnp.exp(-rates_ref[...] * float(BLOCK))
    state = zero_ref[...]
    kept = jnp.ones((8, LANES), f32)
    for b in range(terms_ref.shape[0]):
        factor = live_ref[b : b + 1] * decay
        state = factor * state + terms_ref[b].astype(f32)
        kept = factor * kept
    out_ref[0] = state
    out_ref[1] = kept


def whole(value):
    return pl.BlockSpec(value.shape, lambda *_: (0,) * value.ndim)


def item_spec(tiles):
    return pl.BlockSpec((8, LANES), lambda _, which: (which[0] // tiles, which[0] % tiles))


def make_totals(which, terms, ratesx, live, zero):
    tiles = ratesx.shape[1] // LANES
    return pl.pallas_call(
        totals_kernel,
        out_shape=jax.ShapeDtypeStruct((2, 8, LANES), f32),
        grid_spec=pltpu.PrefetchScalarGridSpec(
            num_scalar_prefetch=1,
            grid=(1,),
            in_specs=[in_vmem(), item_spec(tiles), whole(live), whole(zero)],
            out_specs=in_vmem(),
        ),
        compiler_params=params(),
        name="totals",
    )(which, terms, *hbm(ratesx, live, zero))


def states_kernel(which_ref, terms_ref, rates_ref, live_ref, one_ref, two_ref, out_ref):
    decay = jnp.exp(-rates_ref[...] * float(BLOCK))
    state = one_ref[0] + one_ref[1] * two_ref[...]
    for b in range(terms_ref.shape[0]):
        out_ref[b] = state.astype(bf16)
        state = live_ref[b : b + 1] * decay * state + terms_ref[b].astype(f32)


def make_states(which, terms, ratesx, live, one, two):
    tiles = ratesx.shape[1] // LANES
    return pl.pallas_call(
        states_kernel,
        out_shape=pltpu.HBM(terms.shape, bf16),
        grid_spec=pltpu.PrefetchScalarGridSpec(
            num_scalar_prefetch=1,
            grid=(1,),
            in_specs=[in_vmem(), item_spec(tiles), whole(live), in_vmem(), in_vmem()],
            out_specs=whole(terms),
        ),
        compiler_params=params(),
        name="states",
    )(which, terms, *hbm(ratesx, live), one, two)


def final_kernel(acc_ref, query_ref, dec_ref, state_ref, out_ref):
    same = iota((LANES, LANES), 0) // MODES == iota((LANES, LANES), 1) // GROUP
    keep = jnp.where(same, 1.0, 0.0).astype(bf16)
    for j in range(TILES):
        one = jnp.concatenate([state_ref[0, j], state_ref[1, j]], axis=0)
        spread = jnp.concatenate([one] * PER_TILE, axis=0) * keep
        carried = jnp.dot(dec_ref[:, tile(j)], spread, preferred_element_type=f32)
        filtered = (acc_ref[:, tile(j)] + carried).astype(bf16).astype(f32)
        out_ref[:, tile(j)] = (query_ref[:, tile(j)] * filtered).astype(bf16)


def make_final(acc, query, dec, state):
    return pl.pallas_call(
        final_kernel,
        grid=(acc.shape[1] // WIDE,),
        out_shape=pltpu.HBM(acc.shape, bf16),
        in_specs=[
            columns(BLOCK),
            columns(BLOCK),
            columns(BLOCK),
            pl.BlockSpec((2, TILES, 8, LANES), lambda j: (0, j, 0, 0)),
        ],
        out_specs=columns(BLOCK),
        compiler_params=params(),
        name="final",
    )(*hbm(acc, query, dec), state)


def per_device(projected, doc_lengths, short_taps, medium_taps, decay_rates, residues, skip_gain):
    ts_count = lax.axis_size("ts")
    ctx_count = lax.axis_size("ctx")
    count = ts_count * ctx_count
    ctx = lax.axis_index("ctx")
    index = ctx * ts_count + lax.axis_index("ts")
    size = SPAN * ts_count
    which = (index % size).astype(i32)
    groups = [[s * size + j for j in range(size)] for s in range(count // size)]
    onward = [(i, i + 1) for i in range(count - 1)]
    width = projected.shape[1] // 3

    def from_ctx(value, by):
        return lax.ppermute(value, "ctx", [(i, i + by) for i in range(ctx_count - by)])

    halo = lax.ppermute(projected[BLOCK - 8 :], FLAT, onward)
    place = jnp.concatenate(
        [jnp.stack([index * BLOCK, (index - which) * BLOCK]).astype(i32), doc_lengths]
    )
    scaled = residues * jnp.sqrt(-jnp.expm1(-2.0 * decay_rates))
    taps = jnp.pad(short_taps, ((0, 0), (0, 1), (0, 0))).reshape(24, -1)
    stack = jnp.concatenate([taps, decay_rates, scaled, jnp.zeros_like(taps[:8])], axis=0)
    srel, live, tapsx, ratesx, scalex, tail = make_spread(place, stack, width)
    product, contrib, edge = make_product(projected, halo, tapsx, srel, tail)
    items = contrib.reshape(size, 8, LANES)
    terms = lax.all_to_all(
        items, FLAT, split_axis=0, concat_axis=0, tiled=True, axis_index_groups=groups
    )
    before = lax.ppermute(product, FLAT, onward)
    dec, own, med = make_tables(srel, ratesx, scalex, medium_taps)
    query, acc, zero = make_own(projected, edge, tapsx, srel, product, own, skip_gain.reshape(1, -1))
    ours = which.reshape(1)
    totals = make_totals(ours, terms, ratesx, live, zero)
    one = from_ctx(totals, SPAN)
    two = from_ctx(totals[0], 2 * SPAN)
    states = make_states(ours, terms, ratesx, live, one, two)
    back = lax.all_to_all(
        states, FLAT, split_axis=0, concat_axis=0, tiled=True, axis_index_groups=groups
    )
    acc = make_earlier(before, med, srel, acc)
    return make_final(acc, query, dec, back.reshape(2, width // LANES, 8, LANES))


def solution(mesh):
    return jax.shard_map(
        per_device,
        mesh=mesh,
        in_specs=(P(FLAT, None), P(), P(), P(), P(), P(), P()),
        out_specs=P(FLAT, None),
        check_vma=False,
    )
```

```python
import jax
import jax.numpy as jnp
from jax import lax
from jax.experimental import pallas as pl
from jax.experimental.pallas import tpu as pltpu
from jax.sharding import PartitionSpec as P

GROUP = 16
SHORT = 7
BLOCK = 128
MODES = 16
LANES = 128
DOCS = 16
SPAN = 4
PER_TILE = LANES // GROUP
FLAT = ("ctx", "ts")
HIGHEST = lax.Precision.HIGHEST
f32 = jnp.float32
bf16 = jnp.bfloat16
i32 = jnp.int32


def iota(shape, dim):
    return lax.broadcasted_iota(i32, shape, dim)


TILES = 4
CHUNK = 8
WIDE = CHUNK * LANES


def tile(j):
    if isinstance(j, int):
        return slice(j * LANES, (j + 1) * LANES)
    return pl.ds(pl.multiple_of(j * LANES, LANES), LANES)


def for_tiles(count, body):
    def step(i, carry):
        for j in range(TILES):
            body(i * TILES + j)
        return carry

    lax.fori_loop(0, count // TILES, step, 0)


def in_hbm():
    return pl.BlockSpec(memory_space=pltpu.HBM)


def in_vmem():
    return pl.BlockSpec(memory_space=pltpu.VMEM)


def in_smem():
    return pl.BlockSpec(memory_space=pltpu.SMEM)


def columns(rows, first=0):
    return pl.BlockSpec((rows, WIDE), lambda j: (0, first + j))


def rows_of(count):
    return pl.BlockSpec((count, LANES), lambda j: (j, 0))


def fixed(shape):
    return pl.BlockSpec(shape, lambda j: (0,) * len(shape))


def hbm(*values):
    return [pltpu.with_memory_space_constraint(value, pltpu.HBM) for value in values]


def params(mib=12):
    return pltpu.CompilerParams(vmem_limit_bytes=mib << 20)


def front_kernel(
    place_ref, docs_ref, taps_ref, rates_ref, raw_ref,
    srel_ref, live_ref, tapsx_ref, tail_ref, product_ref, head_ref,
    stack_ref, pieces_ref, raws_ref, wk_ref, wv_ref, sems,
):
    width = product_ref.shape[1]
    copies = [
        pltpu.make_async_copy(
            raw_ref.at[:, pl.ds(width * (1 + p), width)], raws_ref.at[p], sems.at[p]
        )
        for p in range(2)
    ]
    for copy in copies:
        copy.start()
    row = iota((BLOCK, LANES), 0)
    base = place_ref[0]
    pos = base + row
    starts = jnp.zeros((BLOCK, LANES), i32)
    ends = place_ref[1] + row[: live_ref.shape[0]] * BLOCK + (BLOCK - 1)
    lasts = jnp.zeros(live_ref.shape, i32)
    begin = jnp.int32(0)
    for d in range(DOCS):
        starts = jnp.where(pos >= begin, begin, starts)
        lasts = jnp.where(ends >= begin, begin, lasts)
        begin = begin + docs_ref[d]
    srel_ref[...] = starts - base
    live_ref[...] = jnp.where(lasts < ends - (BLOCK - 1), 1.0, 0.0)
    stack_ref[...] = jnp.zeros(stack_ref.shape, f32)
    for p in range(3):
        stack_ref[8 * p : 8 * p + SHORT] = taps_ref[p]
    stack_ref[24:40] = rates_ref[...]
    split_into(pieces_ref, stack_ref[...])
    own_mode = iota((MODES, LANES), 0) == iota((MODES, LANES), 1) % MODES
    behind = (BLOCK - 1 - row).astype(f32)

    def expand(j):
        spread = expanded(pieces_ref, j)
        tapsx_ref[:, tile(j)] = spread[0:24]
        rate = jnp.sum(jnp.where(own_mode, spread[24:40], 0.0), axis=0, keepdims=True)
        tail_ref[tile(j), :] = jnp.exp(-rate * behind).astype(bf16).T

    for_tiles(width // LANES, expand)
    for copy in copies:
        copy.wait()
    rel = row - (starts - base)
    nothing = jnp.zeros((8, LANES), f32)

    def multiply(j):
        slot = lax.rem(j, TILES)
        key = feature_of(raws_ref.at[0], nothing, tapsx_ref, 1, j, rel, wk_ref.at[slot])
        value = feature_of(raws_ref.at[1], nothing, tapsx_ref, 2, j, rel, wv_ref.at[slot])
        product_ref[:, tile(j)] = (key * value).astype(bf16)

    for_tiles(width // LANES, multiply)
    head_ref[0] = raws_ref[0, 0:8]
    head_ref[1] = raws_ref[1, 0:8]


def split_into(pieces_ref, whole):
    upper = whole.astype(bf16)
    rest = whole - upper.astype(f32)
    middle = rest.astype(bf16)
    pieces_ref[0] = upper
    pieces_ref[1] = middle
    pieces_ref[2] = (rest - middle.astype(f32)).astype(bf16)


def expanded(pieces_ref, j):
    _, lines, groups = pieces_ref.shape
    pieces = jnp.concatenate([pieces_ref[0], pieces_ref[1], pieces_ref[2]], axis=0)
    ahead = iota((groups, LANES), 0) - iota((groups, LANES), 1) // GROUP
    hot = jnp.where(ahead == j * PER_TILE, 1.0, 0.0).astype(bf16)
    spread = jnp.dot(pieces, hot, preferred_element_type=f32)
    return spread[0:lines] + spread[lines : 2 * lines] + spread[2 * lines :]


def make_front(place, doc_lengths, short_taps, decay_rates, projected):
    width = projected.shape[1] // 3
    groups = decay_rates.shape[1]
    shape = jax.ShapeDtypeStruct
    return pl.pallas_call(
        front_kernel,
        grid=(1,),
        out_shape=(
            shape((BLOCK, LANES), i32),
            shape((4 * DOCS, LANES), f32),
            shape((24, width), f32),
            shape((width, BLOCK), bf16),
            shape((BLOCK, width), bf16),
            shape((2, 8, width), bf16),
        ),
        in_specs=[
            in_smem(),
            in_smem(),
            fixed(short_taps.shape),
            fixed(decay_rates.shape),
            in_hbm(),
        ],
        out_specs=tuple([in_vmem()] * 6),
        scratch_shapes=[
            pltpu.VMEM((48, groups), f32),
            pltpu.VMEM((3, 48, groups), bf16),
            pltpu.VMEM((2, BLOCK, width), bf16),
            pltpu.VMEM((TILES, 8 + BLOCK, LANES), f32),
            pltpu.VMEM((TILES, 8 + BLOCK, LANES), f32),
            pltpu.SemaphoreType.DMA((2,)),
        ],
        compiler_params=params(),
        name="front",
    )(place, *hbm(doc_lengths, short_taps, decay_rates, projected))


def edge_kernel(
    main_ref, head_ref, halo_ref, taps_ref, srel_ref, live_ref, tail_ref,
    product_out, contrib_out, edge_ref, tapsq_ref, srel_out, live_out,
    window_ref, product_ref, contrib_ref, sems,
):
    width = main_ref.shape[1]
    row = iota((BLOCK, LANES), 0)
    kept = jnp.where(row >= srel_ref[BLOCK - 1 : BLOCK], 1.0, 0.0).astype(bf16)
    rel = (row - srel_ref[...])[0:8]
    lane_group = iota((MODES, LANES), 1) // GROUP
    edge_ref[...] = halo_ref[:, 0:width]
    tapsq_ref[...] = taps_ref[0:8]
    srel_out[...] = srel_ref[...]
    live_out[...] = live_ref[...]

    def body(j):
        slot = lax.rem(j, TILES)
        values = []
        for p in range(2):
            past = halo_ref[:, tile(j + (1 + p) * (width // LANES))].astype(f32)
            window = window_ref.at[slot, p]
            window[0:8] = past
            window[8:16] = head_ref[p, :, tile(j)].astype(f32)
            line = 8 * (p + 1)
            summed = window[8:16] * taps_ref[line : line + 1, tile(j)]
            for offset in range(1, SHORT):
                term = window[8 - offset : 16 - offset]
                term = term * taps_ref[line + offset : line + offset + 1, tile(j)]
                summed = summed + jnp.where(rel >= offset, term, 0.0)
            values.append(summed)
        first = values[0] * values[1]
        rest = main_ref[0:16, tile(j)].astype(f32)[8:16]
        both = jnp.concatenate([first, rest], axis=0).astype(bf16)
        product = jnp.concatenate([both, main_ref[16:BLOCK, tile(j)]], axis=0)
        product_ref[:, tile(j)] = product
        all_modes = jnp.dot(
            tail_ref[tile(j), :], product * kept, preferred_element_type=f32
        )
        contrib = all_modes[0:MODES]
        for g in range(1, PER_TILE):
            contrib = jnp.where(
                lane_group == g, all_modes[g * MODES : (g + 1) * MODES], contrib
            )
        contrib_ref[0, j] = contrib[0:8].astype(bf16)
        contrib_ref[1, j] = contrib[8:16].astype(bf16)

    def copies(c):
        at = pl.ds(pl.multiple_of(c * WIDE, LANES), WIDE)
        tiles = pl.ds(pl.multiple_of(c * CHUNK, CHUNK), CHUNK)
        return (
            pltpu.make_async_copy(product_ref.at[:, at], product_out.at[:, at], sems.at[0, c]),
            pltpu.make_async_copy(contrib_ref.at[:, tiles], contrib_out.at[:, tiles], sems.at[1, c]),
        )

    def chunk(c, carry):
        def inner(i, more):
            for k in range(TILES):
                body(c * CHUNK + i * TILES + k)
            return more

        lax.fori_loop(0, CHUNK // TILES, inner, 0)
        for copy in copies(c):
            copy.start()
        return carry

    chunks = width // WIDE
    lax.fori_loop(0, chunks, chunk, 0)
    for c in range(chunks):
        for copy in copies(c):
            copy.wait()


def make_edge(main, head, halo, tapsx, srel, live, tail):
    width = main.shape[1]
    shape = pltpu.HBM
    return pl.pallas_call(
        edge_kernel,
        out_shape=(
            shape((BLOCK, width), bf16),
            shape((2, width // LANES, 8, LANES), bf16),
            shape((8, width), bf16),
            shape((8, width), f32),
            shape(srel.shape, i32),
            shape(live.shape, f32),
        ),
        in_specs=[in_vmem()] * 7,
        out_specs=(in_hbm(), in_hbm(), in_vmem(), in_vmem(), in_vmem(), in_vmem()),
        scratch_shapes=[
            pltpu.VMEM((TILES, 2, 16, LANES), f32),
            pltpu.VMEM((BLOCK, width), bf16),
            pltpu.VMEM((2, width // LANES, 8, LANES), bf16),
            pltpu.SemaphoreType.DMA((2, width // WIDE)),
        ],
        compiler_params=params(),
        name="edge",
    )(main, head, halo, tapsx, srel, live, tail)


def tables_kernel(
    srel_ref, rates_ref, scaled_ref, medium_ref,
    dec_ref, own_ref, med_ref, ratesx_ref,
    long_ref, pieces_ref,
):
    row = iota((BLOCK, LANES), 0)
    lane = iota((BLOCK, LANES), 1)
    old = srel_ref[...] < 0
    own_mode = iota((MODES, LANES), 0) == iota((MODES, LANES), 1) % MODES
    ahead = (row + 1).astype(f32)
    behind = (BLOCK - 1 - row).astype(f32)
    each = LANES // PER_TILE
    split_into(pieces_ref, jnp.concatenate([rates_ref[...], scaled_ref[...]], axis=0))
    long_ref[...] = jnp.zeros(long_ref.shape, f32)

    def step(i, carry):
        total = long_ref[(i * TILES) // each]
        for k in range(TILES):
            j = i * TILES + k
            spread = expanded(pieces_ref, j)
            ratesx_ref[:, tile(j)] = spread[0:MODES]
            rate = jnp.sum(jnp.where(own_mode, spread[0:MODES], 0.0), axis=0, keepdims=True)
            scale = jnp.sum(jnp.where(own_mode, spread[MODES:], 0.0), axis=0, keepdims=True)
            decay = jnp.where(old, scale * jnp.exp(-rate * ahead), 0.0)
            dec_ref[:, tile(j)] = decay.astype(bf16)
            power = scale * jnp.exp(-rate * behind)
            upper = power.astype(bf16)
            lower = (power - upper.astype(f32)).astype(bf16)
            first = lax.rem(j, each) * PER_TILE
            hot = jnp.where(lane - row // MODES == first, 1.0, 0.0).astype(bf16)
            total = total + jnp.dot(
                jnp.concatenate([upper, lower], axis=1),
                jnp.concatenate([hot, hot], axis=0),
                preferred_element_type=f32,
            )
        long_ref[(i * TILES) // each] = total
        return carry

    lax.fori_loop(0, dec_ref.shape[1] // (LANES * TILES), step, 0)
    flip = jnp.where(row + lane == BLOCK - 1, 1.0, 0.0)
    for h in range(long_ref.shape[0]):
        medium = jnp.dot(
            flip, medium_ref[:, tile(h)], precision=HIGHEST, preferred_element_type=f32
        )
        med_ref[tile(h), :] = medium.T
        own_ref[tile(h), :] = (medium + long_ref[h]).T


def make_tables(srel, decay_rates, scaled, medium_taps, width):
    groups = medium_taps.shape[1]
    shape = jax.ShapeDtypeStruct
    return pl.pallas_call(
        tables_kernel,
        grid=(1,),
        out_shape=(
            pltpu.HBM((BLOCK, width), bf16),
            shape((groups, BLOCK), f32),
            pltpu.HBM((groups, BLOCK), f32),
            shape((MODES, width), f32),
        ),
        in_specs=[
            fixed((BLOCK, LANES)),
            fixed(decay_rates.shape),
            fixed(scaled.shape),
            fixed(medium_taps.shape),
        ],
        out_specs=tuple([in_vmem()] * 4),
        scratch_shapes=[
            pltpu.VMEM((groups // LANES, BLOCK, LANES), f32),
            pltpu.VMEM((3, 2 * MODES, groups), bf16),
        ],
        compiler_params=params(),
        name="tables",
    )(*hbm(srel, decay_rates, scaled, medium_taps))


def feature_of(raw_ref, past, taps_ref, part, j, rel, window_ref):
    window_ref[0:8] = past
    window_ref[8 : 8 + BLOCK] = raw_ref[:, tile(j)].astype(f32)
    summed = window_ref[8 : 8 + BLOCK] * taps_ref[8 * part : 8 * part + 1, tile(j)]
    for offset in range(1, SHORT):
        tap = taps_ref[8 * part + offset : 8 * part + offset + 1, tile(j)]
        term = window_ref[8 - offset : 8 - offset + BLOCK] * tap
        summed = summed + jnp.where(rel >= offset, term, 0.0)
    return summed


def band_sum(j, x_ref, taps_ref, mask_ref, acc):
    lane_group = iota((1, LANES), 1) // GROUP
    even = jnp.where(lane_group % 2 == 0, 1.0, 0.0).astype(bf16)
    odd = jnp.where(lane_group % 2 == 1, 1.0, 0.0).astype(bf16)
    x = x_ref[:, tile(j)]
    both = jnp.concatenate([x * even, x * odd], axis=0)
    pair_of = iota((BLOCK, LANES), 1) // (2 * GROUP)
    taps = taps_ref[pl.ds(pl.multiple_of(j * PER_TILE, PER_TILE), PER_TILE), :]
    pairs = []
    for pair in range(PER_TILE // 2):
        bands = []
        for side in range(2):
            g = 2 * pair + side
            line = jnp.broadcast_to(taps[g : g + 1], (16, BLOCK))
            ring = pltpu.roll(line, 1, 1, stride=1, stride_axis=0).astype(bf16)
            parts = [ring] + [pltpu.roll(ring, 16 * k, 1) for k in range(1, BLOCK // 16)]
            bands.append(jnp.concatenate(parts, axis=0) * mask_ref[...])
        pairs.append(jnp.concatenate(bands, axis=1))
    out = jnp.dot(jnp.concatenate(pairs, axis=0), both, preferred_element_type=f32)
    picked = out[0:BLOCK]
    for pair in range(1, PER_TILE // 2):
        picked = jnp.where(pair_of == pair, out[pair * BLOCK : (pair + 1) * BLOCK], picked)
    return acc + picked


def own_kernel(
    which_ref, q_ref, hq_ref, taps_ref, srel_ref, x_ref, own_ref, skip_ref, rates_ref, live_ref,
    query_ref, acc_ref, decay_ref, live_out,
    wq_ref, mask_ref,
):
    row = iota((BLOCK, LANES), 0)
    lane = iota((BLOCK, LANES), 1)
    rel = row - srel_ref[...]

    @pl.when(pl.program_id(0) == 0)
    def _():
        mask = (lane <= row) & (lane >= srel_ref[...])
        mask_ref[...] = jnp.where(mask, 1.0, 0.0).astype(bf16)
        decay_ref[...] = jnp.exp(-rates_ref[...] * float(BLOCK))
        live_out[...] = live_ref[...]

    def body(j):
        slot = lax.rem(j, TILES)
        past = hq_ref[:, tile(j)].astype(f32)
        query_ref[:, tile(j)] = feature_of(q_ref, past, taps_ref, 0, j, rel, wq_ref.at[slot])
        acc = skip_ref[:, tile(j)] * x_ref[:, tile(j)].astype(f32)
        acc_ref[:, tile(j)] = band_sum(j, x_ref, own_ref, mask_ref, acc)

    for_tiles(CHUNK, body)


def cols(rows, first=0):
    return pl.BlockSpec((rows, WIDE), lambda j, *_: (0, first + j))


def whole(shape):
    return pl.BlockSpec(shape, lambda *_: (0,) * len(shape))


def make_own(which, projected, edge, tapsq, srel, product, own, skip, ratesx, live):
    width = product.shape[1]
    tiles = width // LANES
    shape = jax.ShapeDtypeStruct
    return pl.pallas_call(
        own_kernel,
        out_shape=(
            pltpu.HBM((BLOCK, width), f32),
            pltpu.HBM((BLOCK, width), f32),
            shape((8, LANES), f32),
            shape(live.shape, f32),
        ),
        grid_spec=pltpu.PrefetchScalarGridSpec(
            num_scalar_prefetch=1,
            grid=(width // WIDE,),
            in_specs=[
                cols(BLOCK),
                cols(8),
                cols(8),
                whole((BLOCK, LANES)),
                cols(BLOCK),
                pl.BlockSpec((WIDE // GROUP, LANES), lambda j, *_: (j, 0)),
                cols(1),
                pl.BlockSpec((8, LANES), lambda _, at: (at[0] // tiles, at[0] % tiles)),
                whole(live.shape),
            ],
            out_specs=(
                cols(BLOCK),
                cols(BLOCK),
                whole((8, LANES)),
                whole(live.shape),
            ),
            scratch_shapes=[
                pltpu.VMEM((TILES, 8 + BLOCK, LANES), f32),
                pltpu.VMEM((BLOCK, LANES), bf16),
            ],
        ),
        compiler_params=params(20),
        name="own",
    )(which, *hbm(projected, edge, tapsq, srel, product), own, *hbm(skip), ratesx, *hbm(live))


def earlier_kernel(
    x_ref, taps_ref, srel_ref, acc_ref, dec_ref,
    out_ref, dec_out,
    mask_ref,
):
    row = iota((BLOCK, LANES), 0)
    lane = iota((BLOCK, LANES), 1)
    dec_out[...] = dec_ref[...]

    @pl.when(pl.program_id(0) == 0)
    def _():
        inside = (lane > row) & (lane - BLOCK >= srel_ref[...])
        mask_ref[...] = jnp.where(inside, 1.0, 0.0).astype(bf16)

    def body(j):
        out_ref[:, tile(j)] = band_sum(j, x_ref, taps_ref, mask_ref, acc_ref[:, tile(j)])

    for_tiles(CHUNK, body)


def make_earlier(before, med, srel, acc, dec):
    width = acc.shape[1]
    shape = jax.ShapeDtypeStruct
    return pl.pallas_call(
        earlier_kernel,
        grid=(width // WIDE,),
        out_shape=(
            shape(acc.shape, f32),
            shape(acc.shape, bf16),
        ),
        in_specs=[
            columns(BLOCK),
            rows_of(WIDE // GROUP),
            fixed((BLOCK, LANES)),
            columns(BLOCK),
            columns(BLOCK),
        ],
        out_specs=(columns(BLOCK), columns(BLOCK)),
        scratch_shapes=[pltpu.VMEM((BLOCK, LANES), bf16)],
        compiler_params=params(20),
        name="earlier",
    )(before, *hbm(med, srel, acc, dec))


def totals_kernel(terms_ref, decay_ref, live_ref, out_ref):
    decay = decay_ref[...]
    state = jnp.zeros((8, LANES), f32)
    kept = jnp.ones((8, LANES), f32)
    for b in range(terms_ref.shape[0]):
        factor = live_ref[b : b + 1] * decay
        state = factor * state + terms_ref[b].astype(f32)
        kept = factor * kept
    out_ref[0] = state
    out_ref[1] = kept


def make_totals(terms, decay, live):
    return pl.pallas_call(
        totals_kernel,
        out_shape=jax.ShapeDtypeStruct((2, 8, LANES), f32),
        in_specs=[in_vmem()] * 3,
        out_specs=in_vmem(),
        compiler_params=params(),
        name="totals",
    )(terms, decay, live)


def states_kernel(terms_ref, decay_ref, live_ref, one_ref, two_ref, out_ref):
    decay = decay_ref[...]
    state = one_ref[0] + one_ref[1] * two_ref[0]
    for b in range(terms_ref.shape[0]):
        out_ref[b] = state.astype(bf16)
        state = live_ref[b : b + 1] * decay * state + terms_ref[b].astype(f32)


def make_states(terms, decay, live, one, two):
    return pl.pallas_call(
        states_kernel,
        out_shape=pltpu.HBM(terms.shape, bf16),
        in_specs=[in_vmem()] * 5,
        out_specs=in_vmem(),
        compiler_params=params(),
        name="states",
    )(terms, decay, live, one, two)


def final_kernel(
    acc_ref, query_hbm, dec_ref, state_ref, out_hbm,
    query_ref, filtered_ref, out_ref, sems,
):
    width = acc_ref.shape[1]
    chunks = width // WIDE

    def span(c):
        return pl.ds(pl.multiple_of(c * WIDE, LANES), WIDE)

    def fetch(c):
        return pltpu.make_async_copy(
            query_hbm.at[:, span(c)], query_ref.at[:, span(c)], sems.at[0, c]
        )

    def send(c):
        return pltpu.make_async_copy(
            out_ref.at[:, span(c)], out_hbm.at[:, span(c)], sems.at[1, c]
        )

    for c in range(chunks):
        fetch(c).start()
    same = iota((LANES, LANES), 0) // MODES == iota((LANES, LANES), 1) // GROUP
    keep = jnp.where(same, 1.0, 0.0).astype(bf16)

    def carry_in(j):
        one = jnp.concatenate([state_ref[0, j], state_ref[1, j]], axis=0)
        spread = jnp.concatenate([one] * PER_TILE, axis=0) * keep
        carried = jnp.dot(dec_ref[:, tile(j)], spread, preferred_element_type=f32)
        filtered_ref[:, tile(j)] = (acc_ref[:, tile(j)] + carried).astype(bf16)

    for_tiles(width // LANES, carry_in)

    def chunk(c, carry):
        fetch(c).wait()

        def inner(i, more):
            at = tile(c * CHUNK + i)
            filtered = filtered_ref[:, at].astype(f32)
            out_ref[:, at] = (query_ref[:, at] * filtered).astype(bf16)
            return more

        lax.fori_loop(0, CHUNK, inner, 0)
        send(c).start()
        return carry

    lax.fori_loop(0, chunks, chunk, 0)
    for c in range(chunks):
        send(c).wait()


def make_final(acc, query, dec, state):
    chunks = acc.shape[1] // WIDE
    return pl.pallas_call(
        final_kernel,
        out_shape=pltpu.HBM(acc.shape, bf16),
        in_specs=[in_vmem(), in_hbm(), in_vmem(), in_vmem()],
        out_specs=in_hbm(),
        scratch_shapes=[
            pltpu.VMEM(acc.shape, f32),
            pltpu.VMEM(acc.shape, bf16),
            pltpu.VMEM(acc.shape, bf16),
            pltpu.SemaphoreType.DMA((2, chunks)),
        ],
        compiler_params=params(),
        name="final",
    )(acc, *hbm(query), dec, state)


def per_device(projected, doc_lengths, short_taps, medium_taps, decay_rates, residues, skip_gain):
    ts_count = lax.axis_size("ts")
    ctx_count = lax.axis_size("ctx")
    count = ts_count * ctx_count
    ctx = lax.axis_index("ctx")
    index = ctx * ts_count + lax.axis_index("ts")
    size = SPAN * ts_count
    which = (index % size).astype(i32)
    groups = [[s * size + j for j in range(size)] for s in range(count // size)]
    onward = [(i, i + 1) for i in range(count - 1)]
    width = projected.shape[1] // 3

    def from_ctx(value, by):
        return lax.ppermute(value, "ctx", [(i, i + by) for i in range(ctx_count - by)])

    halo = lax.ppermute(projected[BLOCK - 8 :], FLAT, onward)
    place = jnp.stack([index * BLOCK, (index - which) * BLOCK]).astype(i32)
    srel, live, tapsx, tail, main, head = make_front(
        place, doc_lengths, short_taps, decay_rates, projected
    )
    product, contrib, edge, tapsq, srel, live = make_edge(
        main, head, halo, tapsx, srel, live, tail
    )
    before = lax.ppermute(product, FLAT, onward)
    items = contrib.reshape(size, 8, LANES)
    terms = lax.all_to_all(
        items, FLAT, split_axis=0, concat_axis=0, tiled=True, axis_index_groups=groups
    )
    scaled = residues * jnp.sqrt(-jnp.expm1(-2.0 * decay_rates))
    dec, own, med, ratesx = make_tables(srel, decay_rates, scaled, medium_taps, width)
    query, acc, decay, near = make_own(
        which.reshape(1), projected, edge, tapsq, srel, product, own,
        skip_gain.reshape(1, -1), ratesx, live,
    )
    totals = make_totals(terms, decay, near)
    one = from_ctx(totals, SPAN)
    two = from_ctx(totals, 2 * SPAN)
    states = make_states(terms, decay, near, one, two)
    back = lax.all_to_all(
        states, FLAT, split_axis=0, concat_axis=0, tiled=True, axis_index_groups=groups
    )
    acc, dec = make_earlier(before, med, srel, acc, dec)
    return make_final(acc, query, dec, back.reshape(2, width // LANES, 8, LANES))


def solution(mesh):
    return jax.shard_map(
        per_device,
        mesh=mesh,
        in_specs=(P(FLAT, None), P(), P(), P(), P(), P(), P()),
        out_specs=P(FLAT, None),
        check_vma=False,
    )
```

```python
import jax
import jax.numpy as jnp
from jax import lax
from jax.experimental import pallas as pl
from jax.experimental.pallas import tpu as pltpu
from jax.sharding import PartitionSpec as P

GROUP = 16
SHORT = 7
BLOCK = 128
MODES = 16
LANES = 128
DOCS = 16
SPAN = 8
PARTS = 4
PART = MODES // PARTS
PER_TILE = LANES // GROUP
FLAT = ("ctx", "ts")
HIGHEST = lax.Precision.HIGHEST
f32 = jnp.float32
bf16 = jnp.bfloat16
i32 = jnp.int32


def iota(shape, dim):
    return lax.broadcasted_iota(i32, shape, dim)


TILES = 4
CHUNK = 8
ROWS = 32
WIDE = CHUNK * LANES


def tile(j):
    if isinstance(j, int):
        return slice(j * LANES, (j + 1) * LANES)
    return pl.ds(pl.multiple_of(j * LANES, LANES), LANES)


def for_tiles(count, body, unroll=TILES):
    def step(i, carry):
        for k in range(unroll):
            body(i * unroll + k, k)
        return carry

    lax.fori_loop(0, count // unroll, step, 0)


def in_hbm():
    return pl.BlockSpec(memory_space=pltpu.HBM)


def in_vmem():
    return pl.BlockSpec(memory_space=pltpu.VMEM)


def in_smem():
    return pl.BlockSpec(memory_space=pltpu.SMEM)


def columns(rows, first=0):
    return pl.BlockSpec((rows, WIDE), lambda j: (0, first + j))


def rows_of(count):
    return pl.BlockSpec((count, LANES), lambda j: (j, 0))


def fixed(shape):
    return pl.BlockSpec(shape, lambda j: (0,) * len(shape))


def hbm(*values):
    return [pltpu.with_memory_space_constraint(value, pltpu.HBM) for value in values]


def params(mib=12):
    return pltpu.CompilerParams(vmem_limit_bytes=mib << 20)


def front_kernel(
    place_ref, docs_ref, taps_ref, rates_ref, raw_ref,
    srel_ref, live_ref, tapsx_ref, tail_ref, product_ref, head_ref,
    stack_ref, pieces_ref, raws_ref, wk_ref, wv_ref, rel_ref, near_ref, sems,
):
    width = product_ref.shape[1]
    copies = [
        pltpu.make_async_copy(
            raw_ref.at[:, pl.ds(width * (1 + p), width)], raws_ref.at[p], sems.at[p]
        )
        for p in range(2)
    ]
    for copy in copies:
        copy.start()
    row = iota((BLOCK, LANES), 0)
    base = place_ref[0]
    pos = base + row
    starts = jnp.zeros((BLOCK, LANES), i32)
    ends = place_ref[1] + row[: live_ref.shape[0]] * BLOCK + (BLOCK - 1)
    lasts = jnp.zeros(live_ref.shape, i32)
    begin = jnp.int32(0)
    for d in range(DOCS):
        starts = jnp.where(pos >= begin, begin, starts)
        lasts = jnp.where(ends >= begin, begin, lasts)
        begin = begin + docs_ref[d]
    srel_ref[...] = starts - base
    live_ref[...] = jnp.where(lasts < ends - (BLOCK - 1), 1.0, 0.0)
    stack_ref[...] = jnp.zeros(stack_ref.shape, f32)
    for p in range(3):
        stack_ref[8 * p : 8 * p + SHORT] = taps_ref[p]
    stack_ref[24:40] = rates_ref[...]
    split_into(pieces_ref, stack_ref[...])
    own_mode = iota((MODES, LANES), 0) == iota((MODES, LANES), 1) % MODES
    behind = (BLOCK - 1 - row).astype(f32)

    def expand(j, k):
        spread = expanded(pieces_ref, j)
        tapsx_ref[:, tile(j)] = spread[0:24]
        rate = jnp.sum(jnp.where(own_mode, spread[24:40], 0.0), axis=0, keepdims=True)
        tail_ref[tile(j), :] = jnp.exp(-rate * behind).astype(bf16).T

    for_tiles(width // LANES, expand)
    for copy in copies:
        copy.wait()
    rel_ref[...] = row - (starts - base)
    nothing = jnp.zeros((8, LANES), f32)

    def rows_of_product(at, masked):
        rows = slice(at, at + ROWS)

        def multiply(j, k):
            key = feature_of(
                raws_ref.at[0], nothing, tapsx_ref, 1, j, at, rel_ref, wk_ref.at[k], masked
            )
            value = feature_of(
                raws_ref.at[1], nothing, tapsx_ref, 2, j, at, rel_ref, wv_ref.at[k], masked
            )
            product_ref[rows, tile(j)] = (key * value).astype(bf16)

        for_tiles(width // LANES, multiply)

    in_row_parts(rel_ref, near_ref, rows_of_product)
    head_ref[0] = raws_ref[0, 0:8]
    head_ref[1] = raws_ref[1, 0:8]


def split_into(pieces_ref, whole):
    upper = whole.astype(bf16)
    rest = whole - upper.astype(f32)
    middle = rest.astype(bf16)
    pieces_ref[0] = upper
    pieces_ref[1] = middle
    pieces_ref[2] = (rest - middle.astype(f32)).astype(bf16)


def expanded(pieces_ref, j):
    _, lines, groups = pieces_ref.shape
    pieces = jnp.concatenate([pieces_ref[0], pieces_ref[1], pieces_ref[2]], axis=0)
    ahead = iota((groups, LANES), 0) - iota((groups, LANES), 1) // GROUP
    hot = jnp.where(ahead == j * PER_TILE, 1.0, 0.0).astype(bf16)
    spread = jnp.dot(pieces, hot, preferred_element_type=f32)
    return spread[0:lines] + spread[lines : 2 * lines] + spread[2 * lines :]


def make_front(place, doc_lengths, short_taps, decay_rates, projected, size):
    width = projected.shape[1] // 3
    groups = decay_rates.shape[1]
    shape = jax.ShapeDtypeStruct
    return pl.pallas_call(
        front_kernel,
        grid=(1,),
        out_shape=(
            shape((BLOCK, LANES), i32),
            shape((size, LANES), f32),
            shape((24, width), f32),
            shape((width, BLOCK), bf16),
            shape((BLOCK, width), bf16),
            shape((2, 8, width), bf16),
        ),
        in_specs=[
            in_smem(),
            in_smem(),
            fixed(short_taps.shape),
            fixed(decay_rates.shape),
            in_hbm(),
        ],
        out_specs=tuple([in_vmem()] * 6),
        scratch_shapes=[
            pltpu.VMEM((48, groups), f32),
            pltpu.VMEM((3, 48, groups), bf16),
            pltpu.VMEM((2, BLOCK, width), bf16),
            pltpu.VMEM((TILES, 8 + ROWS, LANES), f32),
            pltpu.VMEM((TILES, 8 + ROWS, LANES), f32),
            pltpu.VMEM((BLOCK, LANES), i32),
            pltpu.SMEM((BLOCK // ROWS,), i32),
            pltpu.SemaphoreType.DMA((2,)),
        ],
        compiler_params=params(),
        name="front",
    )(place, *hbm(doc_lengths, short_taps, decay_rates, projected))


def edge_kernel(
    main_ref, head_ref, halo_ref, taps_ref, srel_ref, live_ref, tail_ref,
    product_out, contrib_out, edge_ref, tapsq_ref, srel_out, live_out,
    window_ref, product_ref, contrib_ref, sems,
):
    width = main_ref.shape[1]
    row = iota((BLOCK, LANES), 0)
    kept = jnp.where(row >= srel_ref[BLOCK - 1 : BLOCK], 1.0, 0.0).astype(bf16)
    rel = (row - srel_ref[...])[0:8]
    lane_group = iota((MODES, LANES), 1) // GROUP
    edge_ref[...] = halo_ref[:, 0:width]
    tapsq_ref[...] = taps_ref[0:8]
    srel_out[...] = srel_ref[...]
    live_out[...] = live_ref[...]

    def body(j, slot):
        values = []
        for p in range(2):
            past = halo_ref[:, tile(j + (1 + p) * (width // LANES))].astype(f32)
            window = window_ref.at[slot, p]
            window[0:8] = past
            window[8:16] = head_ref[p, :, tile(j)].astype(f32)
            line = 8 * (p + 1)
            summed = window[8:16] * taps_ref[line : line + 1, tile(j)]
            for offset in range(1, SHORT):
                term = window[8 - offset : 16 - offset]
                term = term * taps_ref[line + offset : line + offset + 1, tile(j)]
                summed = summed + jnp.where(rel >= offset, term, 0.0)
            values.append(summed)
        first = values[0] * values[1]
        rest = main_ref[0:16, tile(j)].astype(f32)[8:16]
        both = jnp.concatenate([first, rest], axis=0).astype(bf16)
        product = jnp.concatenate([both, main_ref[16:BLOCK, tile(j)]], axis=0)
        product_ref[:, tile(j)] = product
        all_modes = jnp.dot(
            tail_ref[tile(j), :], product * kept, preferred_element_type=f32
        )
        contrib = all_modes[0:MODES]
        for g in range(1, PER_TILE):
            contrib = jnp.where(
                lane_group == g, all_modes[g * MODES : (g + 1) * MODES], contrib
            )
        for p in range(PARTS):
            contrib_ref[p, j] = contrib[p * PART : (p + 1) * PART].astype(bf16)

    def copies(c):
        at = pl.ds(pl.multiple_of(c * WIDE, LANES), WIDE)
        tiles = pl.ds(pl.multiple_of(c * CHUNK, CHUNK), CHUNK)
        return (
            pltpu.make_async_copy(product_ref.at[:, at], product_out.at[:, at], sems.at[0, c]),
            pltpu.make_async_copy(contrib_ref.at[:, tiles], contrib_out.at[:, tiles], sems.at[1, c]),
        )

    def chunk(c, carry):
        def inner(i, more):
            for k in range(TILES):
                body(c * CHUNK + i * TILES + k, k)
            return more

        lax.fori_loop(0, CHUNK // TILES, inner, 0)
        for copy in copies(c):
            copy.start()
        return carry

    chunks = width // WIDE
    lax.fori_loop(0, chunks, chunk, 0)
    for c in range(chunks):
        for copy in copies(c):
            copy.wait()


def make_edge(main, head, halo, tapsx, srel, live, tail):
    width = main.shape[1]
    shape = pltpu.HBM
    return pl.pallas_call(
        edge_kernel,
        out_shape=(
            shape((BLOCK, width), bf16),
            shape((PARTS, width // LANES, PART, LANES), bf16),
            shape((8, width), bf16),
            shape((8, width), f32),
            shape(srel.shape, i32),
            shape(live.shape, f32),
        ),
        in_specs=[in_vmem()] * 7,
        out_specs=(in_hbm(), in_hbm(), in_vmem(), in_vmem(), in_vmem(), in_vmem()),
        scratch_shapes=[
            pltpu.VMEM((TILES, 2, 16, LANES), f32),
            pltpu.VMEM((BLOCK, width), bf16),
            pltpu.VMEM((PARTS, width // LANES, PART, LANES), bf16),
            pltpu.SemaphoreType.DMA((2, width // WIDE)),
        ],
        compiler_params=params(),
        name="edge",
    )(main, head, halo, tapsx, srel, live, tail)


def tables_kernel(
    srel_ref, rates_ref, scaled_ref, medium_ref,
    dec_ref, own_ref, med_ref, ratesx_ref,
    long_ref, pieces_ref,
):
    row = iota((BLOCK, LANES), 0)
    lane = iota((BLOCK, LANES), 1)
    old = srel_ref[...] < 0
    own_mode = iota((MODES, LANES), 0) == iota((MODES, LANES), 1) % MODES
    ahead = (row + 1).astype(f32)
    behind = (BLOCK - 1 - row).astype(f32)
    each = LANES // PER_TILE
    split_into(pieces_ref, jnp.concatenate([rates_ref[...], scaled_ref[...]], axis=0))
    long_ref[...] = jnp.zeros(long_ref.shape, f32)

    def step(i, carry):
        total = long_ref[(i * TILES) // each]
        for k in range(TILES):
            j = i * TILES + k
            spread = expanded(pieces_ref, j)
            ratesx_ref[:, tile(j)] = spread[0:MODES]
            rate = jnp.sum(jnp.where(own_mode, spread[0:MODES], 0.0), axis=0, keepdims=True)
            scale = jnp.sum(jnp.where(own_mode, spread[MODES:], 0.0), axis=0, keepdims=True)
            decay = jnp.where(old, scale * jnp.exp(-rate * ahead), 0.0)
            dec_ref[:, tile(j)] = decay.astype(bf16)
            power = scale * jnp.exp(-rate * behind)
            upper = power.astype(bf16)
            lower = (power - upper.astype(f32)).astype(bf16)
            first = lax.rem(j, each) * PER_TILE
            hot = jnp.where(lane - row // MODES == first, 1.0, 0.0).astype(bf16)
            total = total + jnp.dot(
                jnp.concatenate([upper, lower], axis=1),
                jnp.concatenate([hot, hot], axis=0),
                preferred_element_type=f32,
            )
        long_ref[(i * TILES) // each] = total
        return carry

    lax.fori_loop(0, dec_ref.shape[1] // (LANES * TILES), step, 0)
    flip = jnp.where(row + lane == BLOCK - 1, 1.0, 0.0)
    for h in range(long_ref.shape[0]):
        medium = jnp.dot(
            flip, medium_ref[:, tile(h)], precision=HIGHEST, preferred_element_type=f32
        )
        med_ref[tile(h), :] = medium.T
        own_ref[tile(h), :] = (medium + long_ref[h]).T


def make_tables(srel, decay_rates, scaled, medium_taps, width):
    groups = medium_taps.shape[1]
    shape = jax.ShapeDtypeStruct
    return pl.pallas_call(
        tables_kernel,
        grid=(1,),
        out_shape=(
            pltpu.HBM((BLOCK, width), bf16),
            shape((groups, BLOCK), f32),
            pltpu.HBM((groups, BLOCK), f32),
            shape((MODES, width), f32),
        ),
        in_specs=[
            fixed((BLOCK, LANES)),
            fixed(decay_rates.shape),
            fixed(scaled.shape),
            fixed(medium_taps.shape),
        ],
        out_specs=tuple([in_vmem()] * 4),
        scratch_shapes=[
            pltpu.VMEM((groups // LANES, BLOCK, LANES), f32),
            pltpu.VMEM((3, 2 * MODES, groups), bf16),
        ],
        compiler_params=params(),
        name="tables",
    )(*hbm(srel, decay_rates, scaled, medium_taps))


def find_near(rel_ref, near_ref):
    for r in range(BLOCK // ROWS):
        least = jnp.min(rel_ref[r * ROWS : (r + 1) * ROWS].astype(f32))
        near_ref[r] = (least < SHORT - 1).astype(i32)


def by_rows(near_ref, work):
    for r in range(BLOCK // ROWS):
        near = near_ref[r] != 0
        pl.when(near)(lambda at=r * ROWS: work(at, True))
        pl.when(jnp.logical_not(near))(lambda at=r * ROWS: work(at, False))


def in_row_parts(rel_ref, near_ref, work):
    find_near(rel_ref, near_ref)
    by_rows(near_ref, work)


def feature_of(raw_ref, past, taps_ref, part, j, at, rel_ref, window_ref, masked):
    if at:
        past = raw_ref[at - 16 : at, tile(j)].astype(f32)[8:16]
    window_ref[0:8] = past
    window_ref[8 : 8 + ROWS] = raw_ref[at : at + ROWS, tile(j)].astype(f32)
    summed = window_ref[8 : 8 + ROWS] * taps_ref[8 * part : 8 * part + 1, tile(j)]
    for offset in range(1, SHORT):
        tap = taps_ref[8 * part + offset : 8 * part + offset + 1, tile(j)]
        term = window_ref[8 - offset : 8 - offset + ROWS] * tap
        if masked:
            term = jnp.where(rel_ref[at : at + ROWS] >= offset, term, 0.0)
        summed = summed + term
    return summed


def band_sum(j, x_ref, taps_ref, mask_ref, acc):
    lane_group = iota((1, LANES), 1) // GROUP
    even = jnp.where(lane_group % 2 == 0, 1.0, 0.0).astype(bf16)
    odd = jnp.where(lane_group % 2 == 1, 1.0, 0.0).astype(bf16)
    x = x_ref[:, tile(j)]
    both = jnp.concatenate([x * even, x * odd], axis=0)
    pair_of = iota((BLOCK, LANES), 1) // (2 * GROUP)
    taps = taps_ref[pl.ds(pl.multiple_of(j * PER_TILE, PER_TILE), PER_TILE), :]
    pairs = []
    for pair in range(PER_TILE // 2):
        bands = []
        for side in range(2):
            g = 2 * pair + side
            line = jnp.broadcast_to(taps[g : g + 1], (16, BLOCK))
            ring = pltpu.roll(line, 1, 1, stride=1, stride_axis=0).astype(bf16)
            parts = [ring] + [pltpu.roll(ring, 16 * k, 1) for k in range(1, BLOCK // 16)]
            bands.append(jnp.concatenate(parts, axis=0) * mask_ref[...])
        pairs.append(jnp.concatenate(bands, axis=1))
    out = jnp.dot(jnp.concatenate(pairs, axis=0), both, preferred_element_type=f32)
    picked = out[0:BLOCK]
    for pair in range(1, PER_TILE // 2):
        picked = jnp.where(pair_of == pair, out[pair * BLOCK : (pair + 1) * BLOCK], picked)
    return acc + picked


def own_kernel(
    which_ref, q_ref, hq_ref, taps_ref, srel_ref, x_ref, own_ref, skip_ref, rates_ref, live_ref,
    query_ref, acc_ref, decay_ref, live_out,
    wq_ref, mask_ref, rel_ref, near_ref,
):
    row = iota((BLOCK, LANES), 0)
    lane = iota((BLOCK, LANES), 1)

    @pl.when(pl.program_id(0) == 0)
    def _():
        mask = (lane <= row) & (lane >= srel_ref[...])
        mask_ref[...] = jnp.where(mask, 1.0, 0.0).astype(bf16)
        tiles = pl.num_programs(0) * CHUNK
        upper = lax.rem(which_ref[0] // tiles, 2) == 1
        rates = jnp.where(upper, rates_ref[PART:8], rates_ref[0:PART])
        decay_ref[...] = jnp.exp(-rates * float(BLOCK))
        live_out[...] = live_ref[...]
        rel_ref[...] = row - srel_ref[...]
        find_near(rel_ref, near_ref)

    def rows_of_query(at, masked):
        def ask(j, k):
            past = hq_ref[:, tile(j)].astype(f32)
            query_ref[at : at + ROWS, tile(j)] = feature_of(
                q_ref, past, taps_ref, 0, j, at, rel_ref, wq_ref.at[k], masked
            )

        for_tiles(CHUNK, ask, CHUNK)

    by_rows(near_ref, rows_of_query)

    def body(j, k):
        acc = skip_ref[:, tile(j)] * x_ref[:, tile(j)].astype(f32)
        acc_ref[:, tile(j)] = band_sum(j, x_ref, own_ref, mask_ref, acc)

    for_tiles(CHUNK, body, CHUNK)


def cols(rows, first=0):
    return pl.BlockSpec((rows, WIDE), lambda j, *_: (0, first + j))


def whole(shape):
    return pl.BlockSpec(shape, lambda *_: (0,) * len(shape))


def make_own(which, projected, edge, tapsq, srel, product, own, skip, ratesx, live):
    width = product.shape[1]
    tiles = width // LANES
    shape = jax.ShapeDtypeStruct
    return pl.pallas_call(
        own_kernel,
        out_shape=(
            pltpu.HBM((BLOCK, width), f32),
            pltpu.HBM((BLOCK, width), f32),
            shape((PART, LANES), f32),
            shape(live.shape, f32),
        ),
        grid_spec=pltpu.PrefetchScalarGridSpec(
            num_scalar_prefetch=1,
            grid=(width // WIDE,),
            in_specs=[
                cols(BLOCK),
                cols(8),
                cols(8),
                whole((BLOCK, LANES)),
                cols(BLOCK),
                pl.BlockSpec((WIDE // GROUP, LANES), lambda j, *_: (j, 0)),
                cols(1),
                pl.BlockSpec((8, LANES), lambda _, at: (at[0] // (2 * tiles), at[0] % tiles)),
                whole(live.shape),
            ],
            out_specs=(
                cols(BLOCK),
                cols(BLOCK),
                whole((PART, LANES)),
                whole(live.shape),
            ),
            scratch_shapes=[
                pltpu.VMEM((CHUNK, 8 + ROWS, LANES), f32),
                pltpu.VMEM((BLOCK, LANES), bf16),
                pltpu.VMEM((BLOCK, LANES), i32),
                pltpu.SMEM((BLOCK // ROWS,), i32),
            ],
        ),
        compiler_params=params(20),
        name="own",
    )(which, *hbm(projected, edge, tapsq, srel, product), own, *hbm(skip), ratesx, *hbm(live))


def earlier_kernel(
    x_ref, taps_ref, srel_ref, acc_ref, dec_ref,
    out_ref, dec_out,
    mask_ref,
):
    row = iota((BLOCK, LANES), 0)
    lane = iota((BLOCK, LANES), 1)
    dec_out[...] = dec_ref[...]

    @pl.when(pl.program_id(0) == 0)
    def _():
        inside = (lane > row) & (lane - BLOCK >= srel_ref[...])
        mask_ref[...] = jnp.where(inside, 1.0, 0.0).astype(bf16)

    def body(j, k):
        out_ref[:, tile(j)] = band_sum(j, x_ref, taps_ref, mask_ref, acc_ref[:, tile(j)])

    for_tiles(CHUNK, body, CHUNK)


def make_earlier(before, med, srel, acc, dec):
    width = acc.shape[1]
    shape = jax.ShapeDtypeStruct
    return pl.pallas_call(
        earlier_kernel,
        grid=(width // WIDE,),
        out_shape=(
            shape(acc.shape, f32),
            shape(acc.shape, bf16),
        ),
        in_specs=[
            columns(BLOCK),
            rows_of(WIDE // GROUP),
            fixed((BLOCK, LANES)),
            columns(BLOCK),
            columns(BLOCK),
        ],
        out_specs=(columns(BLOCK), columns(BLOCK)),
        scratch_shapes=[pltpu.VMEM((BLOCK, LANES), bf16)],
        compiler_params=params(20),
        name="earlier",
    )(*hbm(before, med, srel, acc, dec))


def totals_kernel(terms_ref, decay_ref, live_ref, out_ref):
    decay = decay_ref[...]
    state = jnp.zeros((PART, LANES), f32)
    for b in range(terms_ref.shape[0]):
        state = live_ref[b : b + 1] * decay * state + terms_ref[b].astype(f32)
    out_ref[...] = state


def make_totals(terms, decay, live):
    return pl.pallas_call(
        totals_kernel,
        out_shape=jax.ShapeDtypeStruct((PART, LANES), f32),
        in_specs=[in_vmem()] * 3,
        out_specs=in_vmem(),
        compiler_params=params(),
        name="totals",
    )(terms, decay, live)


def states_kernel(terms_ref, decay_ref, live_ref, enter_ref, out_ref):
    decay = decay_ref[...]
    state = enter_ref[...]
    for b in range(terms_ref.shape[0]):
        out_ref[b] = state.astype(bf16)
        state = live_ref[b : b + 1] * decay * state + terms_ref[b].astype(f32)


def make_states(terms, decay, live, enter):
    return pl.pallas_call(
        states_kernel,
        out_shape=pltpu.HBM(terms.shape, bf16),
        in_specs=[in_vmem()] * 4,
        out_specs=in_vmem(),
        compiler_params=params(),
        name="states",
    )(terms, decay, live, enter)


def final_kernel(
    acc_ref, query_hbm, dec_ref, state_ref, out_hbm,
    query_ref, filtered_ref, out_ref, sems,
):
    width = acc_ref.shape[1]
    chunks = width // WIDE

    def span(c):
        return pl.ds(pl.multiple_of(c * WIDE, LANES), WIDE)

    def fetch(c):
        return pltpu.make_async_copy(
            query_hbm.at[:, span(c)], query_ref.at[:, span(c)], sems.at[0, c]
        )

    def send(c):
        return pltpu.make_async_copy(
            out_ref.at[:, span(c)], out_hbm.at[:, span(c)], sems.at[1, c]
        )

    for c in range(chunks):
        fetch(c).start()
    same = iota((LANES, LANES), 0) // MODES == iota((LANES, LANES), 1) // GROUP
    keep = jnp.where(same, 1.0, 0.0).astype(bf16)

    def carry_in(j, k):
        parts = [state_ref[p, j].astype(f32) for p in range(PARTS)]
        one = jnp.concatenate(parts, axis=0).astype(bf16)
        spread = jnp.concatenate([one] * PER_TILE, axis=0) * keep
        carried = jnp.dot(dec_ref[:, tile(j)], spread, preferred_element_type=f32)
        filtered_ref[:, tile(j)] = (acc_ref[:, tile(j)] + carried).astype(bf16)

    for_tiles(width // LANES, carry_in)

    def chunk(c, carry):
        fetch(c).wait()

        def inner(i, more):
            at = tile(c * CHUNK + i)
            filtered = filtered_ref[:, at].astype(f32)
            out_ref[:, at] = (query_ref[:, at] * filtered).astype(bf16)
            return more

        lax.fori_loop(0, CHUNK, inner, 0)
        send(c).start()
        return carry

    lax.fori_loop(0, chunks, chunk, 0)
    for c in range(chunks):
        send(c).wait()


def make_final(acc, query, dec, state):
    chunks = acc.shape[1] // WIDE
    return pl.pallas_call(
        final_kernel,
        out_shape=pltpu.HBM(acc.shape, bf16),
        in_specs=[in_vmem(), in_hbm(), in_vmem(), in_vmem()],
        out_specs=in_hbm(),
        scratch_shapes=[
            pltpu.VMEM(acc.shape, f32),
            pltpu.VMEM(acc.shape, bf16),
            pltpu.VMEM(acc.shape, bf16),
            pltpu.SemaphoreType.DMA((2, chunks)),
        ],
        compiler_params=params(),
        name="final",
    )(acc, *hbm(query), dec, state)


def per_device(projected, doc_lengths, short_taps, medium_taps, decay_rates, residues, skip_gain):
    ts_count = lax.axis_size("ts")
    ctx_count = lax.axis_size("ctx")
    count = ts_count * ctx_count
    ctx = lax.axis_index("ctx")
    index = ctx * ts_count + lax.axis_index("ts")
    size = SPAN * ts_count
    which = (index % size).astype(i32)
    groups = [[s * size + j for j in range(size)] for s in range(count // size)]
    onward = [(i, i + 1) for i in range(count - 1)]
    width = projected.shape[1] // 3

    def from_ctx(value, by):
        return lax.ppermute(value, "ctx", [(i, i + by) for i in range(ctx_count - by)])

    halo = lax.ppermute(projected[BLOCK - 8 :], FLAT, onward)
    place = jnp.stack([index * BLOCK, (index - which) * BLOCK]).astype(i32)
    srel, live, tapsx, tail, main, head = make_front(
        place, doc_lengths, short_taps, decay_rates, projected, size
    )
    product, contrib, edge, tapsq, srel, live = make_edge(
        main, head, halo, tapsx, srel, live, tail
    )
    before = lax.ppermute(product, FLAT, onward)
    items = contrib.reshape(size, PART, LANES)
    terms = lax.all_to_all(
        items, FLAT, split_axis=0, concat_axis=0, tiled=True, axis_index_groups=groups
    )
    scaled = residues * jnp.sqrt(-jnp.expm1(-2.0 * decay_rates))
    dec, own, med, ratesx = make_tables(srel, decay_rates, scaled, medium_taps, width)
    query, acc, decay, near = make_own(
        which.reshape(1), projected, edge, tapsq, srel, product, own,
        skip_gain.reshape(1, -1), ratesx, live,
    )
    totals = make_totals(terms, decay, near)
    enter = from_ctx(totals, SPAN)
    states = make_states(terms, decay, near, enter)
    back = lax.all_to_all(
        states, FLAT, split_axis=0, concat_axis=0, tiled=True, axis_index_groups=groups
    )
    acc, dec = make_earlier(before, med, srel, acc, dec)
    return make_final(acc, query, dec, back.reshape(PARTS, width // LANES, PART, LANES))


def solution(mesh):
    return jax.shard_map(
        per_device,
        mesh=mesh,
        in_specs=(P(FLAT, None), P(), P(), P(), P(), P(), P()),
        out_specs=P(FLAT, None),
        check_vma=False,
    )
```

```python
import jax
import jax.numpy as jnp
from jax import lax
from jax.experimental import pallas as pl
from jax.experimental.pallas import tpu as pltpu
from jax.sharding import PartitionSpec as P

GROUP = 16
SHORT = 7
BLOCK = 128
MODES = 16
LANES = 128
DOCS = 16
SPAN = 4
PARTS = 2
PART = MODES // PARTS
PER_TILE = LANES // GROUP
FLAT = ("ctx", "ts")
HIGHEST = lax.Precision.HIGHEST
f32 = jnp.float32
bf16 = jnp.bfloat16
i32 = jnp.int32


def iota(shape, dim):
    return lax.broadcasted_iota(i32, shape, dim)


TILES = 4
CHUNK = 8
ROWS = 32
WIDE = CHUNK * LANES


def tile(j):
    if isinstance(j, int):
        return slice(j * LANES, (j + 1) * LANES)
    return pl.ds(pl.multiple_of(j * LANES, LANES), LANES)


def for_tiles(count, body, unroll=TILES):
    def step(i, carry):
        for k in range(unroll):
            body(i * unroll + k, k)
        return carry

    lax.fori_loop(0, count // unroll, step, 0)


def in_hbm():
    return pl.BlockSpec(memory_space=pltpu.HBM)


def in_vmem():
    return pl.BlockSpec(memory_space=pltpu.VMEM)


def in_smem():
    return pl.BlockSpec(memory_space=pltpu.SMEM)


def columns(rows, first=0):
    return pl.BlockSpec((rows, WIDE), lambda j: (0, first + j))


def rows_of(count):
    return pl.BlockSpec((count, LANES), lambda j: (j, 0))


def fixed(shape):
    return pl.BlockSpec(shape, lambda j: (0,) * len(shape))


def hbm(*values):
    return [pltpu.with_memory_space_constraint(value, pltpu.HBM) for value in values]


def params(mib=12):
    return pltpu.CompilerParams(vmem_limit_bytes=mib << 20)


def front_kernel(
    place_ref, docs_ref, taps_ref, rates_ref, raw_ref,
    srel_ref, live_ref, tapsx_ref, tail_ref, product_ref, head_ref,
    stack_ref, raws_ref, wk_ref, wv_ref, rel_ref, near_ref, sems,
):
    width = product_ref.shape[1]
    copies = [
        pltpu.make_async_copy(
            raw_ref.at[:, pl.ds(width * (1 + p), width)], raws_ref.at[p], sems.at[p]
        )
        for p in range(2)
    ]
    for copy in copies:
        copy.start()
    row = iota((BLOCK, LANES), 0)
    base = place_ref[0]
    pos = base + row
    starts = jnp.zeros((BLOCK, LANES), i32)
    ends = place_ref[1] + row[: live_ref.shape[0]] * BLOCK + (BLOCK - 1)
    lasts = jnp.zeros(live_ref.shape, i32)
    begin = jnp.int32(0)
    for d in range(DOCS):
        starts = jnp.where(pos >= begin, begin, starts)
        lasts = jnp.where(ends >= begin, begin, lasts)
        begin = begin + docs_ref[d]
    srel_ref[...] = starts - base
    live_ref[...] = jnp.where(lasts < ends - (BLOCK - 1), 1.0, 0.0)
    stack_ref[...] = jnp.zeros(stack_ref.shape, f32)
    for p in range(3):
        stack_ref[8 * p : 8 * p + SHORT] = taps_ref[p]
    stack_ref[24:40] = rates_ref[...]
    own_mode = iota((MODES, LANES), 0) == iota((MODES, LANES), 1) % MODES
    behind = (BLOCK - 1 - row).astype(f32)

    def expand(j, k, half):
        spread = expanded(stack_ref, j, half)
        tapsx_ref[:, tile(j)] = spread[0:24]
        rate = jnp.sum(jnp.where(own_mode, spread[24:40], 0.0), axis=0, keepdims=True)
        tail_ref[tile(j), :] = jnp.exp(-rate * behind).astype(bf16).T

    for_halves(stack_ref.shape[1], expand)
    for copy in copies:
        copy.wait()
    rel_ref[...] = row - (starts - base)
    nothing = jnp.zeros((8, LANES), f32)

    def rows_of_product(at, masked):
        rows = slice(at, at + ROWS)

        def multiply(j, k):
            key = feature_of(
                raws_ref.at[0], nothing, tapsx_ref, 1, j, at, rel_ref, wk_ref.at[k], masked
            )
            value = feature_of(
                raws_ref.at[1], nothing, tapsx_ref, 2, j, at, rel_ref, wv_ref.at[k], masked
            )
            product_ref[rows, tile(j)] = (key * value).astype(bf16)

        for_tiles(width // LANES, multiply)

    in_row_parts(rel_ref, near_ref, rows_of_product)
    head_ref[0] = raws_ref[0, 0:8]
    head_ref[1] = raws_ref[1, 0:8]


def expanded(lines_ref, j, half):
    lines = lines_ref[:, tile(half)]
    first = (j - half * (LANES // PER_TILE)) * PER_TILE
    at = first + iota(lines.shape, 1) // GROUP
    return jnp.take_along_axis(lines, at, axis=1, mode="promise_in_bounds")


def for_halves(groups, body, unroll=TILES):
    each = LANES // PER_TILE
    for half in range(groups // LANES):

        def step(i, carry):
            for k in range(unroll):
                body(half * each + i * unroll + k, k, half)
            return carry

        lax.fori_loop(0, each // unroll, step, 0)


def make_front(place, doc_lengths, short_taps, decay_rates, projected, size):
    width = projected.shape[1] // 3
    groups = decay_rates.shape[1]
    shape = jax.ShapeDtypeStruct
    return pl.pallas_call(
        front_kernel,
        grid=(1,),
        out_shape=(
            shape((BLOCK, LANES), i32),
            shape((size, LANES), f32),
            shape((24, width), f32),
            shape((width, BLOCK), bf16),
            shape((BLOCK, width), bf16),
            shape((2, 8, width), bf16),
        ),
        in_specs=[
            in_smem(),
            in_smem(),
            fixed(short_taps.shape),
            fixed(decay_rates.shape),
            in_hbm(),
        ],
        out_specs=tuple([in_vmem()] * 6),
        scratch_shapes=[
            pltpu.VMEM((40, groups), f32),
            pltpu.VMEM((2, BLOCK, width), bf16),
            pltpu.VMEM((TILES, 8 + ROWS, LANES), f32),
            pltpu.VMEM((TILES, 8 + ROWS, LANES), f32),
            pltpu.VMEM((BLOCK, LANES), i32),
            pltpu.SMEM((BLOCK // ROWS,), i32),
            pltpu.SemaphoreType.DMA((2,)),
        ],
        compiler_params=params(),
        name="front",
    )(place, *hbm(doc_lengths, short_taps, decay_rates, projected))


def edge_kernel(
    main_ref, head_ref, halo_ref, taps_ref, srel_ref, live_ref, tail_ref,
    product_out, contrib_out, edge_ref, tapsq_ref, srel_out, live_out,
    window_ref, product_ref, contrib_ref, sems,
):
    width = main_ref.shape[1]
    row = iota((BLOCK, LANES), 0)
    kept = jnp.where(row >= srel_ref[BLOCK - 1 : BLOCK], 1.0, 0.0).astype(bf16)
    rel = (row - srel_ref[...])[0:8]
    lane_group = iota((MODES, LANES), 1) // GROUP
    edge_ref[...] = halo_ref[:, 0:width]
    tapsq_ref[...] = taps_ref[0:8]
    srel_out[...] = srel_ref[...]
    live_out[...] = live_ref[...]

    def body(j, slot):
        values = []
        for p in range(2):
            past = halo_ref[:, tile(j + (1 + p) * (width // LANES))].astype(f32)
            window = window_ref.at[slot, p]
            window[0:8] = past
            window[8:16] = head_ref[p, :, tile(j)].astype(f32)
            line = 8 * (p + 1)
            summed = window[8:16] * taps_ref[line : line + 1, tile(j)]
            for offset in range(1, SHORT):
                term = window[8 - offset : 16 - offset]
                term = term * taps_ref[line + offset : line + offset + 1, tile(j)]
                summed = summed + jnp.where(rel >= offset, term, 0.0)
            values.append(summed)
        first = values[0] * values[1]
        rest = main_ref[0:16, tile(j)].astype(f32)[8:16]
        both = jnp.concatenate([first, rest], axis=0).astype(bf16)
        product = jnp.concatenate([both, main_ref[16:BLOCK, tile(j)]], axis=0)
        product_ref[:, tile(j)] = product
        all_modes = jnp.dot(
            tail_ref[tile(j), :], product * kept, preferred_element_type=f32
        )
        contrib = all_modes[0:MODES]
        for g in range(1, PER_TILE):
            contrib = jnp.where(
                lane_group == g, all_modes[g * MODES : (g + 1) * MODES], contrib
            )
        for p in range(PARTS):
            contrib_ref[p, j] = contrib[p * PART : (p + 1) * PART].astype(bf16)

    def copies(c):
        at = pl.ds(pl.multiple_of(c * WIDE, LANES), WIDE)
        tiles = pl.ds(pl.multiple_of(c * CHUNK, CHUNK), CHUNK)
        return (
            pltpu.make_async_copy(product_ref.at[:, at], product_out.at[:, at], sems.at[0, c]),
            pltpu.make_async_copy(contrib_ref.at[:, tiles], contrib_out.at[:, tiles], sems.at[1, c]),
        )

    def chunk(c, carry):
        def inner(i, more):
            for k in range(TILES):
                body(c * CHUNK + i * TILES + k, k)
            return more

        lax.fori_loop(0, CHUNK // TILES, inner, 0)
        for copy in copies(c):
            copy.start()
        return carry

    chunks = width // WIDE
    lax.fori_loop(0, chunks, chunk, 0)
    for c in range(chunks):
        for copy in copies(c):
            copy.wait()


def make_edge(main, head, halo, tapsx, srel, live, tail):
    width = main.shape[1]
    shape = pltpu.HBM
    return pl.pallas_call(
        edge_kernel,
        out_shape=(
            shape((BLOCK, width), bf16),
            shape((PARTS, width // LANES, PART, LANES), bf16),
            shape((8, width), bf16),
            shape((8, width), f32),
            shape(srel.shape, i32),
            shape(live.shape, f32),
        ),
        in_specs=[in_vmem()] * 7,
        out_specs=(in_hbm(), in_hbm(), in_vmem(), in_vmem(), in_vmem(), in_vmem()),
        scratch_shapes=[
            pltpu.VMEM((TILES, 2, 16, LANES), f32),
            pltpu.VMEM((BLOCK, width), bf16),
            pltpu.VMEM((PARTS, width // LANES, PART, LANES), bf16),
            pltpu.SemaphoreType.DMA((2, width // WIDE)),
        ],
        compiler_params=params(),
        name="edge",
    )(main, head, halo, tapsx, srel, live, tail)


def tables_kernel(
    srel_ref, rates_ref, scaled_ref, medium_ref,
    dec_ref, own_ref, med_ref, ratesx_ref,
    long_ref, lines_ref,
):
    row = iota((BLOCK, LANES), 0)
    lane = iota((BLOCK, LANES), 1)
    old = srel_ref[...] < 0
    own_mode = iota((MODES, LANES), 0) == iota((MODES, LANES), 1) % MODES
    ahead = (row + 1).astype(f32)
    behind = (BLOCK - 1 - row).astype(f32)
    lines_ref[0:MODES] = rates_ref[...]
    lines_ref[MODES:] = scaled_ref[...]
    long_ref[...] = jnp.zeros(long_ref.shape, f32)
    ahead_of = lane - row // MODES

    def body(j, k, half):
        spread = expanded(lines_ref, j, half)
        ratesx_ref[:, tile(j)] = spread[0:MODES]
        rate = jnp.sum(jnp.where(own_mode, spread[0:MODES], 0.0), axis=0, keepdims=True)
        scale = jnp.sum(jnp.where(own_mode, spread[MODES:], 0.0), axis=0, keepdims=True)
        decay = jnp.where(old, scale * jnp.exp(-rate * ahead), 0.0)
        dec_ref[:, tile(j)] = decay.astype(bf16)
        power = scale * jnp.exp(-rate * behind)
        upper = power.astype(bf16)
        lower = (power - upper.astype(f32)).astype(bf16)
        first = (j - half * (LANES // PER_TILE)) * PER_TILE
        hot = jnp.where(ahead_of == first, 1.0, 0.0).astype(bf16)
        long_ref[half] += jnp.dot(
            jnp.concatenate([upper, lower], axis=1),
            jnp.concatenate([hot, hot], axis=0),
            preferred_element_type=f32,
        )

    for_halves(medium_ref.shape[1], body)
    flip = jnp.where(row + lane == BLOCK - 1, 1.0, 0.0)
    for h in range(long_ref.shape[0]):
        medium = jnp.dot(
            flip, medium_ref[:, tile(h)], precision=HIGHEST, preferred_element_type=f32
        )
        med_ref[tile(h), :] = medium.T
        own_ref[tile(h), :] = (medium + long_ref[h]).T


def make_tables(srel, decay_rates, scaled, medium_taps, width):
    groups = medium_taps.shape[1]
    shape = jax.ShapeDtypeStruct
    return pl.pallas_call(
        tables_kernel,
        grid=(1,),
        out_shape=(
            pltpu.HBM((BLOCK, width), bf16),
            shape((groups, BLOCK), f32),
            pltpu.HBM((groups, BLOCK), f32),
            shape((MODES, width), f32),
        ),
        in_specs=[
            fixed((BLOCK, LANES)),
            fixed(decay_rates.shape),
            fixed(scaled.shape),
            fixed(medium_taps.shape),
        ],
        out_specs=tuple([in_vmem()] * 4),
        scratch_shapes=[
            pltpu.VMEM((groups // LANES, BLOCK, LANES), f32),
            pltpu.VMEM((2 * MODES, groups), f32),
        ],
        compiler_params=params(),
        name="tables",
    )(*hbm(srel, decay_rates, scaled, medium_taps))


def find_near(rel_ref, near_ref):
    for r in range(BLOCK // ROWS):
        least = jnp.min(rel_ref[r * ROWS : (r + 1) * ROWS].astype(f32))
        near_ref[r] = (least < SHORT - 1).astype(i32)


def by_rows(near_ref, work):
    for r in range(BLOCK // ROWS):
        near = near_ref[r] != 0
        pl.when(near)(lambda at=r * ROWS: work(at, True))
        pl.when(jnp.logical_not(near))(lambda at=r * ROWS: work(at, False))


def in_row_parts(rel_ref, near_ref, work):
    find_near(rel_ref, near_ref)
    by_rows(near_ref, work)


def feature_of(raw_ref, past, taps_ref, part, j, at, rel_ref, window_ref, masked):
    if at:
        past = raw_ref[at - 16 : at, tile(j)].astype(f32)[8:16]
    window_ref[0:8] = past
    window_ref[8 : 8 + ROWS] = raw_ref[at : at + ROWS, tile(j)].astype(f32)
    summed = window_ref[8 : 8 + ROWS] * taps_ref[8 * part : 8 * part + 1, tile(j)]
    for offset in range(1, SHORT):
        tap = taps_ref[8 * part + offset : 8 * part + offset + 1, tile(j)]
        term = window_ref[8 - offset : 8 - offset + ROWS] * tap
        if masked:
            term = jnp.where(rel_ref[at : at + ROWS] >= offset, term, 0.0)
        summed = summed + term
    return summed


def band_sum(j, x_ref, taps_ref, mask_ref, acc):
    lane_group = iota((1, LANES), 1) // GROUP
    even = jnp.where(lane_group % 2 == 0, 1.0, 0.0).astype(bf16)
    odd = jnp.where(lane_group % 2 == 1, 1.0, 0.0).astype(bf16)
    x = x_ref[:, tile(j)]
    both = jnp.concatenate([x * even, x * odd], axis=0)
    pair_of = iota((BLOCK, LANES), 1) // (2 * GROUP)
    taps = taps_ref[pl.ds(pl.multiple_of(j * PER_TILE, PER_TILE), PER_TILE), :]
    pairs = []
    for pair in range(PER_TILE // 2):
        bands = []
        for side in range(2):
            g = 2 * pair + side
            line = jnp.broadcast_to(taps[g : g + 1], (16, BLOCK))
            ring = pltpu.roll(line, 1, 1, stride=1, stride_axis=0).astype(bf16)
            parts = [ring] + [pltpu.roll(ring, 16 * k, 1) for k in range(1, BLOCK // 16)]
            bands.append(jnp.concatenate(parts, axis=0) * mask_ref[...])
        pairs.append(jnp.concatenate(bands, axis=1))
    out = jnp.dot(jnp.concatenate(pairs, axis=0), both, preferred_element_type=f32)
    picked = out[0:BLOCK]
    for pair in range(1, PER_TILE // 2):
        picked = jnp.where(pair_of == pair, out[pair * BLOCK : (pair + 1) * BLOCK], picked)
    return acc + picked


def own_kernel(
    which_ref, srel_ref, x_ref, own_ref, skip_ref, rates_ref, live_ref,
    acc_ref, decay_ref, live_out,
    mask_ref,
):
    row = iota((BLOCK, LANES), 0)
    lane = iota((BLOCK, LANES), 1)

    @pl.when(pl.program_id(0) == 0)
    def _():
        mask = (lane <= row) & (lane >= srel_ref[...])
        mask_ref[...] = jnp.where(mask, 1.0, 0.0).astype(bf16)
        decay_ref[...] = jnp.exp(-rates_ref[...] * float(BLOCK))
        live_out[...] = live_ref[...]

    def body(j, k):
        acc = skip_ref[:, tile(j)] * x_ref[:, tile(j)].astype(f32)
        acc_ref[:, tile(j)] = band_sum(j, x_ref, own_ref, mask_ref, acc)

    for_tiles(CHUNK, body, CHUNK)


def cols(rows, first=0):
    return pl.BlockSpec((rows, WIDE), lambda j, *_: (0, first + j))


def whole(shape):
    return pl.BlockSpec(shape, lambda *_: (0,) * len(shape))


def make_own(which, srel, product, own, skip, ratesx, live):
    width = product.shape[1]
    tiles = width // LANES
    shape = jax.ShapeDtypeStruct
    return pl.pallas_call(
        own_kernel,
        out_shape=(
            pltpu.HBM((BLOCK, width), f32),
            shape((PART, LANES), f32),
            shape(live.shape, f32),
        ),
        grid_spec=pltpu.PrefetchScalarGridSpec(
            num_scalar_prefetch=1,
            grid=(width // WIDE,),
            in_specs=[
                whole((BLOCK, LANES)),
                cols(BLOCK),
                pl.BlockSpec((WIDE // GROUP, LANES), lambda j, *_: (j, 0)),
                cols(1),
                pl.BlockSpec((8, LANES), lambda _, at: (at[0] // tiles, at[0] % tiles)),
                whole(live.shape),
            ],
            out_specs=(cols(BLOCK), whole((PART, LANES)), whole(live.shape)),
            scratch_shapes=[pltpu.VMEM((BLOCK, LANES), bf16)],
        ),
        compiler_params=params(20),
        name="own",
    )(which, *hbm(srel, product), own, *hbm(skip), ratesx, *hbm(live))


def earlier_kernel(
    q_ref, hq_ref, tapsq_ref, x_ref, taps_ref, srel_ref, acc_ref, dec_ref,
    out_ref, dec_out, query_ref,
    mask_ref, wq_ref, rel_ref, near_ref,
):
    row = iota((BLOCK, LANES), 0)
    lane = iota((BLOCK, LANES), 1)
    dec_out[...] = dec_ref[...]

    @pl.when(pl.program_id(0) == 0)
    def _():
        inside = (lane > row) & (lane - BLOCK >= srel_ref[...])
        mask_ref[...] = jnp.where(inside, 1.0, 0.0).astype(bf16)
        rel_ref[...] = row - srel_ref[...]
        find_near(rel_ref, near_ref)

    def rows_of_query(at, masked):
        def ask(j, k):
            past = hq_ref[:, tile(j)].astype(f32)
            query_ref[at : at + ROWS, tile(j)] = feature_of(
                q_ref, past, tapsq_ref, 0, j, at, rel_ref, wq_ref.at[k], masked
            )

        for_tiles(CHUNK, ask, CHUNK)

    by_rows(near_ref, rows_of_query)

    def body(j, k):
        out_ref[:, tile(j)] = band_sum(j, x_ref, taps_ref, mask_ref, acc_ref[:, tile(j)])

    for_tiles(CHUNK, body, CHUNK)


def make_earlier(projected, edge, tapsq, before, med, srel, acc, dec):
    width = acc.shape[1]
    shape = jax.ShapeDtypeStruct
    return pl.pallas_call(
        earlier_kernel,
        grid=(width // WIDE,),
        out_shape=(
            shape(acc.shape, f32),
            shape(acc.shape, bf16),
            pltpu.HBM(acc.shape, f32),
        ),
        in_specs=[
            columns(BLOCK),
            columns(8),
            columns(8),
            columns(BLOCK),
            rows_of(WIDE // GROUP),
            fixed((BLOCK, LANES)),
            columns(BLOCK),
            columns(BLOCK),
        ],
        out_specs=(columns(BLOCK), columns(BLOCK), columns(BLOCK)),
        scratch_shapes=[
            pltpu.VMEM((BLOCK, LANES), bf16),
            pltpu.VMEM((CHUNK, 8 + ROWS, LANES), f32),
            pltpu.VMEM((BLOCK, LANES), i32),
            pltpu.SMEM((BLOCK // ROWS,), i32),
        ],
        compiler_params=params(20),
        name="earlier",
    )(*hbm(projected, edge, tapsq, before, med, srel, acc, dec))


def totals_kernel(terms_ref, decay_ref, live_ref, out_ref):
    decay = decay_ref[...]
    state = jnp.zeros((PART, LANES), f32)
    kept = jnp.ones((PART, LANES), f32)
    for b in range(terms_ref.shape[0]):
        factor = live_ref[b : b + 1] * decay
        state = factor * state + terms_ref[b].astype(f32)
        kept = factor * kept
    out_ref[0] = state
    out_ref[1] = kept


def make_totals(terms, decay, live):
    return pl.pallas_call(
        totals_kernel,
        out_shape=jax.ShapeDtypeStruct((2, PART, LANES), f32),
        in_specs=[in_vmem()] * 3,
        out_specs=in_vmem(),
        compiler_params=params(),
        name="totals",
    )(terms, decay, live)


def states_kernel(terms_ref, decay_ref, live_ref, one_ref, two_ref, out_ref):
    decay = decay_ref[...]
    state = one_ref[0] + one_ref[1] * two_ref[0]
    for b in range(terms_ref.shape[0]):
        out_ref[b] = state.astype(bf16)
        state = live_ref[b : b + 1] * decay * state + terms_ref[b].astype(f32)


def make_states(terms, decay, live, one, two):
    return pl.pallas_call(
        states_kernel,
        out_shape=pltpu.HBM(terms.shape, bf16),
        in_specs=[in_vmem()] * 5,
        out_specs=in_vmem(),
        compiler_params=params(),
        name="states",
    )(terms, decay, live, one, two)


def final_kernel(
    acc_ref, query_hbm, dec_ref, state_ref, out_hbm,
    query_ref, filtered_ref, out_ref, sems,
):
    width = acc_ref.shape[1]
    chunks = width // WIDE

    def span(c):
        return pl.ds(pl.multiple_of(c * WIDE, LANES), WIDE)

    def fetch(c):
        return pltpu.make_async_copy(
            query_hbm.at[:, span(c)], query_ref.at[:, span(c)], sems.at[0, c]
        )

    def send(c):
        return pltpu.make_async_copy(
            out_ref.at[:, span(c)], out_hbm.at[:, span(c)], sems.at[1, c]
        )

    for c in range(chunks):
        fetch(c).start()
    same = iota((LANES, LANES), 0) // MODES == iota((LANES, LANES), 1) // GROUP
    keep = jnp.where(same, 1.0, 0.0).astype(bf16)

    def carry_in(j, k):
        one = jnp.concatenate([state_ref[p, j] for p in range(PARTS)], axis=0)
        spread = jnp.concatenate([one] * PER_TILE, axis=0) * keep
        carried = jnp.dot(dec_ref[:, tile(j)], spread, preferred_element_type=f32)
        filtered_ref[:, tile(j)] = (acc_ref[:, tile(j)] + carried).astype(bf16)

    for_tiles(width // LANES, carry_in)

    def chunk(c, carry):
        fetch(c).wait()

        def inner(j, k):
            at = tile(c * CHUNK + j)
            filtered = filtered_ref[:, at].astype(f32)
            out_ref[:, at] = (query_ref[:, at] * filtered).astype(bf16)

        for_tiles(CHUNK, inner)
        send(c).start()
        return carry

    lax.fori_loop(0, chunks, chunk, 0)
    for c in range(chunks):
        send(c).wait()


def make_final(acc, query, dec, state):
    chunks = acc.shape[1] // WIDE
    return pl.pallas_call(
        final_kernel,
        out_shape=pltpu.HBM(acc.shape, bf16),
        in_specs=[in_vmem(), in_hbm(), in_vmem(), in_vmem()],
        out_specs=in_hbm(),
        scratch_shapes=[
            pltpu.VMEM(acc.shape, f32),
            pltpu.VMEM(acc.shape, bf16),
            pltpu.VMEM(acc.shape, bf16),
            pltpu.SemaphoreType.DMA((2, chunks)),
        ],
        compiler_params=params(),
        name="final",
    )(acc, *hbm(query), dec, state)


def per_device(projected, doc_lengths, short_taps, medium_taps, decay_rates, residues, skip_gain):
    ts_count = lax.axis_size("ts")
    ctx_count = lax.axis_size("ctx")
    count = ts_count * ctx_count
    ctx = lax.axis_index("ctx")
    index = ctx * ts_count + lax.axis_index("ts")
    size = SPAN * ts_count
    which = (index % size).astype(i32)
    groups = [[s * size + j for j in range(size)] for s in range(count // size)]
    onward = [(i, i + 1) for i in range(count - 1)]
    width = projected.shape[1] // 3

    def from_ctx(value, by):
        return lax.ppermute(value, "ctx", [(i, i + by) for i in range(ctx_count - by)])

    halo = lax.ppermute(projected[BLOCK - 8 :], FLAT, onward)
    place = jnp.stack([index * BLOCK, (index - which) * BLOCK]).astype(i32)
    srel, live, tapsx, tail, main, head = make_front(
        place, doc_lengths, short_taps, decay_rates, projected, size
    )
    product, contrib, edge, tapsq, srel, live = make_edge(
        main, head, halo, tapsx, srel, live, tail
    )
    before = lax.ppermute(product, FLAT, onward)
    items = contrib.reshape(size, PART, LANES)
    terms = lax.all_to_all(
        items, FLAT, split_axis=0, concat_axis=0, tiled=True, axis_index_groups=groups
    )
    scaled = residues * jnp.sqrt(-jnp.expm1(-2.0 * decay_rates))
    dec, own, med, ratesx = make_tables(srel, decay_rates, scaled, medium_taps, width)
    acc, decay, near = make_own(
        which.reshape(1), srel, product, own, skip_gain.reshape(1, -1), ratesx, live
    )
    totals = make_totals(terms, decay, near)
    one = from_ctx(totals, SPAN)
    two = from_ctx(totals, 2 * SPAN)
    states = make_states(terms, decay, near, one, two)
    back = lax.all_to_all(
        states, FLAT, split_axis=0, concat_axis=0, tiled=True, axis_index_groups=groups
    )
    acc, dec, query = make_earlier(projected, edge, tapsq, before, med, srel, acc, dec)
    return make_final(acc, query, dec, back.reshape(PARTS, width // LANES, PART, LANES))


def solution(mesh):
    return jax.shard_map(
        per_device,
        mesh=mesh,
        in_specs=(P(FLAT, None), P(), P(), P(), P(), P(), P()),
        out_specs=P(FLAT, None),
        check_vma=False,
    )
```

```python
import jax
import jax.numpy as jnp
from jax import lax
from jax.experimental import pallas as pl
from jax.experimental.pallas import tpu as pltpu
from jax.sharding import PartitionSpec as P

GROUP = 16
SHORT = 7
BLOCK = 128
MODES = 16
LANES = 128
DOCS = 16
SPAN = 4
PARTS = 2
PART = MODES // PARTS
PER_TILE = LANES // GROUP
FLAT = ("ctx", "ts")
HIGHEST = lax.Precision.HIGHEST
f32 = jnp.float32
bf16 = jnp.bfloat16
i32 = jnp.int32


def iota(shape, dim):
    return lax.broadcasted_iota(i32, shape, dim)


TILES = 4
CHUNK = 8
ROWS = 32
WIDE = CHUNK * LANES


def tile(j):
    if isinstance(j, int):
        return slice(j * LANES, (j + 1) * LANES)
    return pl.ds(pl.multiple_of(j * LANES, LANES), LANES)


def for_tiles(count, body, unroll=TILES):
    def step(i, carry):
        for k in range(unroll):
            body(i * unroll + k, k)
        return carry

    lax.fori_loop(0, count // unroll, step, 0)


def in_hbm():
    return pl.BlockSpec(memory_space=pltpu.HBM)


def in_vmem():
    return pl.BlockSpec(memory_space=pltpu.VMEM)


def in_smem():
    return pl.BlockSpec(memory_space=pltpu.SMEM)


def columns(rows, first=0):
    return pl.BlockSpec((rows, WIDE), lambda j: (0, first + j))


def rows_of(count):
    return pl.BlockSpec((count, LANES), lambda j: (j, 0))


def fixed(shape):
    return pl.BlockSpec(shape, lambda j: (0,) * len(shape))


def hbm(*values):
    return [pltpu.with_memory_space_constraint(value, pltpu.HBM) for value in values]


def params(mib=12):
    return pltpu.CompilerParams(vmem_limit_bytes=mib << 20)


def front_kernel(
    place_ref, docs_ref, taps_ref, rates_ref, raw_ref,
    srel_ref, live_ref, tapsx_ref, tail_ref, product_ref, head_ref,
    stack_ref, raws_ref, wk_ref, wv_ref, rel_ref, near_ref, sems,
):
    width = product_ref.shape[1]
    copies = [
        pltpu.make_async_copy(
            raw_ref.at[:, pl.ds(width * (1 + p), width)], raws_ref.at[p], sems.at[p]
        )
        for p in range(2)
    ]
    for copy in copies:
        copy.start()
    row = iota((BLOCK, LANES), 0)
    base = place_ref[0]
    pos = base + row
    starts = jnp.zeros((BLOCK, LANES), i32)
    ends = place_ref[1] + row[: live_ref.shape[0]] * BLOCK + (BLOCK - 1)
    lasts = jnp.zeros(live_ref.shape, i32)
    begin = jnp.int32(0)
    for d in range(DOCS):
        starts = jnp.where(pos >= begin, begin, starts)
        lasts = jnp.where(ends >= begin, begin, lasts)
        begin = begin + docs_ref[d]
    srel_ref[...] = starts - base
    live_ref[...] = jnp.where(lasts < ends - (BLOCK - 1), 1.0, 0.0)
    stack_ref[...] = jnp.zeros(stack_ref.shape, f32)
    for p in range(3):
        stack_ref[8 * p : 8 * p + SHORT] = taps_ref[p]
    stack_ref[24:40] = rates_ref[...]
    own_mode = iota((MODES, LANES), 0) == iota((MODES, LANES), 1) % MODES
    behind = (BLOCK - 1 - row).astype(f32)

    def expand(j, k, half):
        spread = expanded(stack_ref, j, half)
        tapsx_ref[:, tile(j)] = spread[0:24]
        rate = jnp.sum(jnp.where(own_mode, spread[24:40], 0.0), axis=0, keepdims=True)
        tail_ref[tile(j), :] = jnp.exp(-rate * behind).astype(bf16).T

    for_halves(stack_ref.shape[1], expand)
    for copy in copies:
        copy.wait()
    rel_ref[...] = row - (starts - base)
    nothing = jnp.zeros((8, LANES), f32)

    def rows_of_product(at, masked):
        rows = slice(at, at + ROWS)

        def multiply(j, k):
            key = feature_of(
                raws_ref.at[0], nothing, tapsx_ref, 1, j, at, rel_ref, wk_ref.at[k], masked
            )
            value = feature_of(
                raws_ref.at[1], nothing, tapsx_ref, 2, j, at, rel_ref, wv_ref.at[k], masked
            )
            product_ref[rows, tile(j)] = (key * value).astype(bf16)

        for_tiles(width // LANES, multiply)

    in_row_parts(rel_ref, near_ref, rows_of_product)
    head_ref[0] = raws_ref[0, 0:8]
    head_ref[1] = raws_ref[1, 0:8]


def expanded(lines_ref, j, half):
    lines = lines_ref[:, tile(half)]
    first = (j - half * (LANES // PER_TILE)) * PER_TILE
    at = first + iota(lines.shape, 1) // GROUP
    return jnp.take_along_axis(lines, at, axis=1, mode="promise_in_bounds")


def for_halves(groups, body, unroll=TILES):
    each = LANES // PER_TILE
    for half in range(groups // LANES):

        def step(i, carry):
            for k in range(unroll):
                body(half * each + i * unroll + k, k, half)
            return carry

        lax.fori_loop(0, each // unroll, step, 0)


def make_front(place, doc_lengths, short_taps, decay_rates, projected, size):
    width = projected.shape[1] // 3
    groups = decay_rates.shape[1]
    shape = jax.ShapeDtypeStruct
    return pl.pallas_call(
        front_kernel,
        grid=(1,),
        out_shape=(
            shape((BLOCK, LANES), i32),
            shape((size, LANES), f32),
            shape((24, width), f32),
            shape((width, BLOCK), bf16),
            shape((BLOCK, width), bf16),
            shape((2, 8, width), bf16),
        ),
        in_specs=[
            in_smem(),
            in_smem(),
            fixed(short_taps.shape),
            fixed(decay_rates.shape),
            in_hbm(),
        ],
        out_specs=tuple([in_vmem()] * 6),
        scratch_shapes=[
            pltpu.VMEM((40, groups), f32),
            pltpu.VMEM((2, BLOCK, width), bf16),
            pltpu.VMEM((TILES, 8 + ROWS, LANES), f32),
            pltpu.VMEM((TILES, 8 + ROWS, LANES), f32),
            pltpu.VMEM((BLOCK, LANES), i32),
            pltpu.SMEM((BLOCK // ROWS,), i32),
            pltpu.SemaphoreType.DMA((2,)),
        ],
        compiler_params=params(),
        name="front",
    )(place, *hbm(doc_lengths, short_taps, decay_rates, projected))


def edge_kernel(
    main_ref, head_ref, halo_ref, taps_ref, srel_ref, live_ref, tail_ref,
    product_out, contrib_out, edge_out, tapsq_out, srel_out, live_out,
    window_ref, product_ref, contrib_ref, sems, pass_sems,
):
    width = main_ref.shape[1]
    row = iota((BLOCK, LANES), 0)
    kept = jnp.where(row >= srel_ref[BLOCK - 1 : BLOCK], 1.0, 0.0).astype(bf16)
    rel = (row - srel_ref[...])[0:8]
    lane_group = iota((MODES, LANES), 1) // GROUP
    passed = [
        pltpu.make_async_copy(halo_ref.at[:, 0:width], edge_out, pass_sems.at[0]),
        pltpu.make_async_copy(taps_ref.at[0:8], tapsq_out, pass_sems.at[1]),
        pltpu.make_async_copy(srel_ref, srel_out, pass_sems.at[2]),
        pltpu.make_async_copy(live_ref, live_out, pass_sems.at[3]),
    ]
    for copy in passed:
        copy.start()

    def body(j, slot):
        values = []
        for p in range(2):
            past = halo_ref[:, tile(j + (1 + p) * (width // LANES))].astype(f32)
            window = window_ref.at[slot, p]
            window[0:8] = past
            window[8:16] = head_ref[p, :, tile(j)].astype(f32)
            line = 8 * (p + 1)
            summed = window[8:16] * taps_ref[line : line + 1, tile(j)]
            for offset in range(1, SHORT):
                term = window[8 - offset : 16 - offset]
                term = term * taps_ref[line + offset : line + offset + 1, tile(j)]
                summed = summed + jnp.where(rel >= offset, term, 0.0)
            values.append(summed)
        first = values[0] * values[1]
        rest = main_ref[0:16, tile(j)].astype(f32)[8:16]
        both = jnp.concatenate([first, rest], axis=0).astype(bf16)
        product = jnp.concatenate([both, main_ref[16:BLOCK, tile(j)]], axis=0)
        product_ref[:, tile(j)] = product
        all_modes = jnp.dot(
            tail_ref[tile(j), :], product * kept, preferred_element_type=f32
        )
        contrib = all_modes[0:MODES]
        for g in range(1, PER_TILE):
            contrib = jnp.where(
                lane_group == g, all_modes[g * MODES : (g + 1) * MODES], contrib
            )
        for p in range(PARTS):
            contrib_ref[p, j] = contrib[p * PART : (p + 1) * PART].astype(bf16)

    def copies(c):
        at = pl.ds(pl.multiple_of(c * WIDE, LANES), WIDE)
        tiles = pl.ds(pl.multiple_of(c * CHUNK, CHUNK), CHUNK)
        return (
            pltpu.make_async_copy(product_ref.at[:, at], product_out.at[:, at], sems.at[0, c]),
            pltpu.make_async_copy(contrib_ref.at[:, tiles], contrib_out.at[:, tiles], sems.at[1, c]),
        )

    def chunk(c, carry):
        def inner(i, more):
            for k in range(TILES):
                body(c * CHUNK + i * TILES + k, k)
            return more

        lax.fori_loop(0, CHUNK // TILES, inner, 0)
        for copy in copies(c):
            copy.start()
        return carry

    chunks = width // WIDE
    lax.fori_loop(0, chunks, chunk, 0)
    for copy in passed:
        copy.wait()
    for c in range(chunks):
        for copy in copies(c):
            copy.wait()


def make_edge(main, head, halo, tapsx, srel, live, tail):
    width = main.shape[1]
    shape = pltpu.HBM
    return pl.pallas_call(
        edge_kernel,
        out_shape=(
            shape((BLOCK, width), bf16),
            shape((PARTS, width // LANES, PART, LANES), bf16),
            shape((8, width), bf16),
            shape((8, width), f32),
            shape(srel.shape, i32),
            shape(live.shape, f32),
        ),
        in_specs=[in_vmem()] * 7,
        out_specs=tuple([in_hbm()] * 6),
        scratch_shapes=[
            pltpu.VMEM((TILES, 2, 16, LANES), f32),
            pltpu.VMEM((BLOCK, width), bf16),
            pltpu.VMEM((PARTS, width // LANES, PART, LANES), bf16),
            pltpu.SemaphoreType.DMA((2, width // WIDE)),
            pltpu.SemaphoreType.DMA((4,)),
        ],
        compiler_params=params(),
        name="edge",
    )(main, head, halo, tapsx, srel, live, tail)


def tables_kernel(
    srel_ref, rates_ref, scaled_ref, medium_ref,
    dec_ref, own_ref, med_ref, ratesx_ref,
    long_ref, lines_ref,
):
    row = iota((BLOCK, LANES), 0)
    lane = iota((BLOCK, LANES), 1)
    old = srel_ref[...] < 0
    own_mode = iota((MODES, LANES), 0) == iota((MODES, LANES), 1) % MODES
    ahead = (row + 1).astype(f32)
    behind = (BLOCK - 1 - row).astype(f32)
    lines_ref[0:MODES] = rates_ref[...]
    lines_ref[MODES:] = scaled_ref[...]
    long_ref[...] = jnp.zeros(long_ref.shape, f32)
    ahead_of = lane - row // MODES

    def body(j, k, half):
        spread = expanded(lines_ref, j, half)
        ratesx_ref[:, tile(j)] = spread[0:MODES]
        rate = jnp.sum(jnp.where(own_mode, spread[0:MODES], 0.0), axis=0, keepdims=True)
        scale = jnp.sum(jnp.where(own_mode, spread[MODES:], 0.0), axis=0, keepdims=True)
        decay = jnp.where(old, scale * jnp.exp(-rate * ahead), 0.0)
        dec_ref[:, tile(j)] = decay.astype(bf16)
        power = scale * jnp.exp(-rate * behind)
        upper = power.astype(bf16)
        lower = (power - upper.astype(f32)).astype(bf16)
        first = (j - half * (LANES // PER_TILE)) * PER_TILE
        hot = jnp.where(ahead_of == first, 1.0, 0.0).astype(bf16)
        long_ref[half] += jnp.dot(
            jnp.concatenate([upper, lower], axis=1),
            jnp.concatenate([hot, hot], axis=0),
            preferred_element_type=f32,
        )

    for_halves(medium_ref.shape[1], body)
    flip = jnp.where(row + lane == BLOCK - 1, 1.0, 0.0)
    for h in range(long_ref.shape[0]):
        medium = jnp.dot(
            flip, medium_ref[:, tile(h)], precision=HIGHEST, preferred_element_type=f32
        )
        med_ref[tile(h), :] = medium.T
        own_ref[tile(h), :] = (medium + long_ref[h]).T


def make_tables(srel, decay_rates, scaled, medium_taps, width):
    groups = medium_taps.shape[1]
    shape = jax.ShapeDtypeStruct
    return pl.pallas_call(
        tables_kernel,
        grid=(1,),
        out_shape=(
            pltpu.HBM((BLOCK, width), bf16),
            shape((groups, BLOCK), f32),
            pltpu.HBM((groups, BLOCK), f32),
            shape((MODES, width), f32),
        ),
        in_specs=[
            fixed((BLOCK, LANES)),
            fixed(decay_rates.shape),
            fixed(scaled.shape),
            fixed(medium_taps.shape),
        ],
        out_specs=tuple([in_vmem()] * 4),
        scratch_shapes=[
            pltpu.VMEM((groups // LANES, BLOCK, LANES), f32),
            pltpu.VMEM((2 * MODES, groups), f32),
        ],
        compiler_params=params(),
        name="tables",
    )(*hbm(srel, decay_rates, scaled, medium_taps))


def find_near(rel_ref, near_ref):
    for r in range(BLOCK // ROWS):
        least = jnp.min(rel_ref[r * ROWS : (r + 1) * ROWS].astype(f32))
        near_ref[r] = (least < SHORT - 1).astype(i32)


def by_rows(near_ref, work):
    for r in range(BLOCK // ROWS):
        near = near_ref[r] != 0
        pl.when(near)(lambda at=r * ROWS: work(at, True))
        pl.when(jnp.logical_not(near))(lambda at=r * ROWS: work(at, False))


def in_row_parts(rel_ref, near_ref, work):
    find_near(rel_ref, near_ref)
    by_rows(near_ref, work)


def feature_of(raw_ref, past, taps_ref, part, j, at, rel_ref, window_ref, masked):
    if at:
        past = raw_ref[at - 16 : at, tile(j)].astype(f32)[8:16]
    window_ref[0:8] = past
    window_ref[8 : 8 + ROWS] = raw_ref[at : at + ROWS, tile(j)].astype(f32)
    summed = window_ref[8 : 8 + ROWS] * taps_ref[8 * part : 8 * part + 1, tile(j)]
    for offset in range(1, SHORT):
        tap = taps_ref[8 * part + offset : 8 * part + offset + 1, tile(j)]
        term = window_ref[8 - offset : 8 - offset + ROWS] * tap
        if masked:
            term = jnp.where(rel_ref[at : at + ROWS] >= offset, term, 0.0)
        summed = summed + term
    return summed


def band_sum(j, x_ref, taps_ref, mask_ref, acc):
    lane_group = iota((1, LANES), 1) // GROUP
    even = jnp.where(lane_group % 2 == 0, 1.0, 0.0).astype(bf16)
    odd = jnp.where(lane_group % 2 == 1, 1.0, 0.0).astype(bf16)
    x = x_ref[:, tile(j)]
    both = jnp.concatenate([x * even, x * odd], axis=0)
    pair_of = iota((BLOCK, LANES), 1) // (2 * GROUP)
    taps = taps_ref[pl.ds(pl.multiple_of(j * PER_TILE, PER_TILE), PER_TILE), :]
    pairs = []
    for pair in range(PER_TILE // 2):
        bands = []
        for side in range(2):
            g = 2 * pair + side
            line = jnp.broadcast_to(taps[g : g + 1], (16, BLOCK))
            ring = pltpu.roll(line, 1, 1, stride=1, stride_axis=0).astype(bf16)
            parts = [ring] + [pltpu.roll(ring, 16 * k, 1) for k in range(1, BLOCK // 16)]
            bands.append(jnp.concatenate(parts, axis=0) * mask_ref[...])
        pairs.append(jnp.concatenate(bands, axis=1))
    out = jnp.dot(jnp.concatenate(pairs, axis=0), both, preferred_element_type=f32)
    picked = out[0:BLOCK]
    for pair in range(1, PER_TILE // 2):
        picked = jnp.where(pair_of == pair, out[pair * BLOCK : (pair + 1) * BLOCK], picked)
    return acc + picked


def own_kernel(
    which_ref, srel_ref, x_ref, own_ref, skip_ref, rates_ref, live_ref,
    acc_ref, decay_ref, live_out,
    mask_ref,
):
    row = iota((BLOCK, LANES), 0)
    lane = iota((BLOCK, LANES), 1)

    @pl.when(pl.program_id(0) == 0)
    def _():
        mask = (lane <= row) & (lane >= srel_ref[...])
        mask_ref[...] = jnp.where(mask, 1.0, 0.0).astype(bf16)
        decay_ref[...] = jnp.exp(-rates_ref[...] * float(BLOCK))
        live_out[...] = live_ref[...]

    def body(j, k):
        acc = skip_ref[:, tile(j)] * x_ref[:, tile(j)].astype(f32)
        acc_ref[:, tile(j)] = band_sum(j, x_ref, own_ref, mask_ref, acc)

    for_tiles(CHUNK, body, CHUNK)


def cols(rows, first=0):
    return pl.BlockSpec((rows, WIDE), lambda j, *_: (0, first + j))


def whole(shape):
    return pl.BlockSpec(shape, lambda *_: (0,) * len(shape))


def make_own(which, srel, product, own, skip, ratesx, live):
    width = product.shape[1]
    tiles = width // LANES
    shape = jax.ShapeDtypeStruct
    return pl.pallas_call(
        own_kernel,
        out_shape=(
            pltpu.HBM((BLOCK, width), f32),
            shape((PART, LANES), f32),
            shape(live.shape, f32),
        ),
        grid_spec=pltpu.PrefetchScalarGridSpec(
            num_scalar_prefetch=1,
            grid=(width // WIDE,),
            in_specs=[
                whole((BLOCK, LANES)),
                cols(BLOCK),
                pl.BlockSpec((WIDE // GROUP, LANES), lambda j, *_: (j, 0)),
                cols(1),
                pl.BlockSpec((8, LANES), lambda _, at: (at[0] // tiles, at[0] % tiles)),
                whole(live.shape),
            ],
            out_specs=(cols(BLOCK), whole((PART, LANES)), whole(live.shape)),
            scratch_shapes=[pltpu.VMEM((BLOCK, LANES), bf16)],
        ),
        compiler_params=params(20),
        name="own",
    )(which, *hbm(srel, product), own, *hbm(skip), ratesx, *hbm(live))


def earlier_kernel(
    q_ref, hq_ref, tapsq_ref, x_ref, taps_ref, srel_ref, acc_ref, dec_ref,
    out_ref, dec_out, query_ref,
    mask_ref, wq_ref, rel_ref, near_ref,
):
    row = iota((BLOCK, LANES), 0)
    lane = iota((BLOCK, LANES), 1)
    dec_out[...] = dec_ref[...]

    @pl.when(pl.program_id(0) == 0)
    def _():
        inside = (lane > row) & (lane - BLOCK >= srel_ref[...])
        mask_ref[...] = jnp.where(inside, 1.0, 0.0).astype(bf16)
        rel_ref[...] = row - srel_ref[...]
        find_near(rel_ref, near_ref)

    def rows_of_query(at, masked):
        def ask(j, k):
            past = hq_ref[:, tile(j)].astype(f32)
            query_ref[at : at + ROWS, tile(j)] = feature_of(
                q_ref, past, tapsq_ref, 0, j, at, rel_ref, wq_ref.at[k], masked
            )

        for_tiles(CHUNK, ask, CHUNK)

    by_rows(near_ref, rows_of_query)

    def body(j, k):
        out_ref[:, tile(j)] = band_sum(j, x_ref, taps_ref, mask_ref, acc_ref[:, tile(j)])

    for_tiles(CHUNK, body, CHUNK)


def make_earlier(projected, edge, tapsq, before, med, srel, acc, dec):
    width = acc.shape[1]
    shape = jax.ShapeDtypeStruct
    return pl.pallas_call(
        earlier_kernel,
        grid=(width // WIDE,),
        out_shape=(
            shape(acc.shape, f32),
            shape(acc.shape, bf16),
            pltpu.HBM(acc.shape, f32),
        ),
        in_specs=[
            columns(BLOCK),
            columns(8),
            columns(8),
            columns(BLOCK),
            rows_of(WIDE // GROUP),
            fixed((BLOCK, LANES)),
            columns(BLOCK),
            columns(BLOCK),
        ],
        out_specs=(columns(BLOCK), columns(BLOCK), columns(BLOCK)),
        scratch_shapes=[
            pltpu.VMEM((BLOCK, LANES), bf16),
            pltpu.VMEM((CHUNK, 8 + ROWS, LANES), f32),
            pltpu.VMEM((BLOCK, LANES), i32),
            pltpu.SMEM((BLOCK // ROWS,), i32),
        ],
        compiler_params=params(20),
        name="earlier",
    )(*hbm(projected, edge, tapsq, before, med, srel, acc, dec))


def totals_kernel(terms_ref, decay_ref, live_ref, out_ref):
    decay = decay_ref[...]
    state = jnp.zeros((PART, LANES), f32)
    kept = jnp.ones((PART, LANES), f32)
    for b in range(terms_ref.shape[0]):
        factor = live_ref[b : b + 1] * decay
        state = factor * state + terms_ref[b].astype(f32)
        kept = factor * kept
    out_ref[0] = state
    out_ref[1] = kept


def make_totals(terms, decay, live):
    return pl.pallas_call(
        totals_kernel,
        out_shape=jax.ShapeDtypeStruct((2, PART, LANES), f32),
        in_specs=[in_vmem()] * 3,
        out_specs=in_vmem(),
        compiler_params=params(),
        name="totals",
    )(terms, decay, live)


def states_kernel(terms_ref, decay_ref, live_ref, one_ref, two_ref, out_ref):
    decay = decay_ref[...]
    state = one_ref[0] + one_ref[1] * two_ref[0]
    for b in range(terms_ref.shape[0]):
        out_ref[b] = state.astype(bf16)
        state = live_ref[b : b + 1] * decay * state + terms_ref[b].astype(f32)


def make_states(terms, decay, live, one, two):
    return pl.pallas_call(
        states_kernel,
        out_shape=pltpu.HBM(terms.shape, bf16),
        in_specs=[in_vmem()] * 5,
        out_specs=in_vmem(),
        compiler_params=params(),
        name="states",
    )(terms, decay, live, one, two)


def final_kernel(
    acc_ref, query_hbm, dec_ref, state_ref, out_hbm,
    query_ref, filtered_ref, out_ref, sems,
):
    width = acc_ref.shape[1]
    chunks = width // WIDE

    def span(c):
        return pl.ds(pl.multiple_of(c * WIDE, LANES), WIDE)

    def fetch(c):
        return pltpu.make_async_copy(
            query_hbm.at[:, span(c)], query_ref.at[:, span(c)], sems.at[0, c]
        )

    def send(c):
        return pltpu.make_async_copy(
            out_ref.at[:, span(c)], out_hbm.at[:, span(c)], sems.at[1, c]
        )

    for c in range(chunks):
        fetch(c).start()
    same = iota((LANES, LANES), 0) // MODES == iota((LANES, LANES), 1) // GROUP
    keep = jnp.where(same, 1.0, 0.0).astype(bf16)

    def carry_in(j, k):
        one = jnp.concatenate([state_ref[p, j] for p in range(PARTS)], axis=0)
        spread = jnp.concatenate([one] * PER_TILE, axis=0) * keep
        carried = jnp.dot(dec_ref[:, tile(j)], spread, preferred_element_type=f32)
        filtered_ref[:, tile(j)] = (acc_ref[:, tile(j)] + carried).astype(bf16)

    for_tiles(width // LANES, carry_in)

    def chunk(c, carry):
        fetch(c).wait()

        def inner(j, k):
            at = tile(c * CHUNK + j)
            filtered = filtered_ref[:, at].astype(f32)
            out_ref[:, at] = (query_ref[:, at] * filtered).astype(bf16)

        for_tiles(CHUNK, inner)
        send(c).start()
        return carry

    lax.fori_loop(0, chunks, chunk, 0)
    for c in range(chunks):
        send(c).wait()


def make_final(acc, query, dec, state):
    chunks = acc.shape[1] // WIDE
    return pl.pallas_call(
        final_kernel,
        out_shape=pltpu.HBM(acc.shape, bf16),
        in_specs=[in_vmem(), in_hbm(), in_vmem(), in_vmem()],
        out_specs=in_hbm(),
        scratch_shapes=[
            pltpu.VMEM(acc.shape, f32),
            pltpu.VMEM(acc.shape, bf16),
            pltpu.VMEM(acc.shape, bf16),
            pltpu.SemaphoreType.DMA((2, chunks)),
        ],
        compiler_params=params(),
        name="final",
    )(acc, *hbm(query), dec, state)


def per_device(projected, doc_lengths, short_taps, medium_taps, decay_rates, residues, skip_gain):
    ts_count = lax.axis_size("ts")
    ctx_count = lax.axis_size("ctx")
    count = ts_count * ctx_count
    ctx = lax.axis_index("ctx")
    index = ctx * ts_count + lax.axis_index("ts")
    size = SPAN * ts_count
    which = (index % size).astype(i32)
    groups = [[s * size + j for j in range(size)] for s in range(count // size)]
    onward = [(i, i + 1) for i in range(count - 1)]
    width = projected.shape[1] // 3

    def from_ctx(value, by):
        return lax.ppermute(value, "ctx", [(i, i + by) for i in range(ctx_count - by)])

    halo = lax.ppermute(projected[BLOCK - 8 :], FLAT, onward)
    place = jnp.stack([index * BLOCK, (index - which) * BLOCK]).astype(i32)
    srel, live, tapsx, tail, main, head = make_front(
        place, doc_lengths, short_taps, decay_rates, projected, size
    )
    product, contrib, edge, tapsq, srel, live = make_edge(
        main, head, halo, tapsx, srel, live, tail
    )
    items = contrib.reshape(size, PART, LANES)
    terms = lax.all_to_all(
        items, FLAT, split_axis=0, concat_axis=0, tiled=True, axis_index_groups=groups
    )
    before = lax.ppermute(product, FLAT, onward)
    scaled = residues * jnp.sqrt(-jnp.expm1(-2.0 * decay_rates))
    dec, own, med, ratesx = make_tables(srel, decay_rates, scaled, medium_taps, width)
    acc, decay, near = make_own(
        which.reshape(1), srel, product, own, skip_gain.reshape(1, -1), ratesx, live
    )
    totals = make_totals(terms, decay, near)
    one = from_ctx(totals, SPAN)
    two = from_ctx(totals, 2 * SPAN)
    states = make_states(terms, decay, near, one, two)
    back = lax.all_to_all(
        states, FLAT, split_axis=0, concat_axis=0, tiled=True, axis_index_groups=groups
    )
    acc, dec, query = make_earlier(projected, edge, tapsq, before, med, srel, acc, dec)
    return make_final(acc, query, dec, back.reshape(PARTS, width // LANES, PART, LANES))


def solution(mesh):
    return jax.shard_map(
        per_device,
        mesh=mesh,
        in_specs=(P(FLAT, None), P(), P(), P(), P(), P(), P()),
        out_specs=P(FLAT, None),
        check_vma=False,
    )
```

```python
import jax
import jax.numpy as jnp
from jax import lax
from jax.experimental import pallas as pl
from jax.experimental.pallas import tpu as pltpu
from jax.sharding import PartitionSpec as P

GROUP = 16
SHORT = 7
BLOCK = 128
MODES = 16
LANES = 128
DOCS = 16
SPAN = 4
PARTS = 2
PART = MODES // PARTS
PER_TILE = LANES // GROUP
FLAT = ("ctx", "ts")
HIGHEST = lax.Precision.HIGHEST
f32 = jnp.float32
bf16 = jnp.bfloat16
i32 = jnp.int32


def iota(shape, dim):
    return lax.broadcasted_iota(i32, shape, dim)


TILES = 4
CHUNK = 8
ROWS = 32
WIDE = CHUNK * LANES


def tile(j):
    if isinstance(j, int):
        return slice(j * LANES, (j + 1) * LANES)
    return pl.ds(pl.multiple_of(j * LANES, LANES), LANES)


def for_tiles(count, body, unroll=TILES):
    def step(i, carry):
        for k in range(unroll):
            body(i * unroll + k, k)
        return carry

    lax.fori_loop(0, count // unroll, step, 0)


def in_hbm():
    return pl.BlockSpec(memory_space=pltpu.HBM)


def in_vmem():
    return pl.BlockSpec(memory_space=pltpu.VMEM)


def in_smem():
    return pl.BlockSpec(memory_space=pltpu.SMEM)


def columns(rows, first=0):
    return pl.BlockSpec((rows, WIDE), lambda j: (0, first + j))


def rows_of(count):
    return pl.BlockSpec((count, LANES), lambda j: (j, 0))


def fixed(shape):
    return pl.BlockSpec(shape, lambda j: (0,) * len(shape))


def hbm(*values):
    return [pltpu.with_memory_space_constraint(value, pltpu.HBM) for value in values]


def params(mib=12):
    return pltpu.CompilerParams(vmem_limit_bytes=mib << 20)


def run_of(first, step, falling):
    blocks = [first]
    for _ in range(BLOCK // 8 - 1):
        blocks.append(blocks[-1] * step)
    return jnp.concatenate(blocks[::-1] if falling else blocks, axis=0)


def front_kernel(
    place_ref, docs_ref, taps_ref, rates_ref, raw_ref,
    srel_ref, live_ref, tapsx_ref, tail_ref, product_ref, head_ref,
    stack_ref, raws_ref, wk_ref, wv_ref, rel_ref, near_ref, sems,
):
    width = product_ref.shape[1]
    copies = [
        pltpu.make_async_copy(
            raw_ref.at[:, pl.ds(width * (1 + p), width)], raws_ref.at[p], sems.at[p]
        )
        for p in range(2)
    ]
    for copy in copies:
        copy.start()
    row = iota((BLOCK, LANES), 0)
    base = place_ref[0]
    pos = base + row
    starts = jnp.zeros((BLOCK, LANES), i32)
    ends = place_ref[1] + row[: live_ref.shape[0]] * BLOCK + (BLOCK - 1)
    lasts = jnp.zeros(live_ref.shape, i32)
    begin = jnp.int32(0)
    for d in range(DOCS):
        starts = jnp.where(pos >= begin, begin, starts)
        lasts = jnp.where(ends >= begin, begin, lasts)
        begin = begin + docs_ref[d]
    srel_ref[...] = starts - base
    live_ref[...] = jnp.where(lasts < ends - (BLOCK - 1), 1.0, 0.0)
    stack_ref[...] = jnp.zeros(stack_ref.shape, f32)
    for p in range(3):
        stack_ref[8 * p : 8 * p + SHORT] = taps_ref[p]
    stack_ref[24:40] = rates_ref[...]
    own_mode = iota((MODES, LANES), 0) == iota((MODES, LANES), 1) % MODES
    behind = (7 - iota((8, LANES), 0)).astype(f32)

    def expand(j, k, half):
        spread = expanded(stack_ref, j, half)
        tapsx_ref[:, tile(j)] = spread[0:24]
        rate = jnp.sum(jnp.where(own_mode, spread[24:40], 0.0), axis=0, keepdims=True)
        power = run_of(jnp.exp(-rate * behind), jnp.exp(-8.0 * rate), True)
        tail_ref[tile(j), :] = power.astype(bf16).T

    for_halves(stack_ref.shape[1], expand)
    for copy in copies:
        copy.wait()
    rel_ref[...] = row - (starts - base)
    nothing = jnp.zeros((8, LANES), f32)

    def rows_of_product(at, masked):
        rows = slice(at, at + ROWS)

        def multiply(j, k):
            key = feature_of(
                raws_ref.at[0], nothing, tapsx_ref, 1, j, at, rel_ref, wk_ref.at[k], masked
            )
            value = feature_of(
                raws_ref.at[1], nothing, tapsx_ref, 2, j, at, rel_ref, wv_ref.at[k], masked
            )
            product_ref[rows, tile(j)] = (key * value).astype(bf16)

        for_tiles(width // LANES, multiply)

    in_row_parts(rel_ref, near_ref, rows_of_product)
    head_ref[0] = raws_ref[0, 0:8]
    head_ref[1] = raws_ref[1, 0:8]


def expanded(lines_ref, j, half):
    lines = lines_ref[:, tile(half)]
    first = (j - half * (LANES // PER_TILE)) * PER_TILE
    at = first + iota(lines.shape, 1) // GROUP
    return jnp.take_along_axis(lines, at, axis=1, mode="promise_in_bounds")


def for_halves(groups, body, unroll=TILES):
    each = LANES // PER_TILE
    for half in range(groups // LANES):

        def step(i, carry):
            for k in range(unroll):
                body(half * each + i * unroll + k, k, half)
            return carry

        lax.fori_loop(0, each // unroll, step, 0)


def make_front(place, doc_lengths, short_taps, decay_rates, projected, size):
    width = projected.shape[1] // 3
    groups = decay_rates.shape[1]
    shape = jax.ShapeDtypeStruct
    return pl.pallas_call(
        front_kernel,
        grid=(1,),
        out_shape=(
            shape((BLOCK, LANES), i32),
            shape((size, LANES), f32),
            shape((24, width), f32),
            shape((width, BLOCK), bf16),
            shape((BLOCK, width), bf16),
            shape((2, 8, width), bf16),
        ),
        in_specs=[
            in_smem(),
            in_smem(),
            fixed(short_taps.shape),
            fixed(decay_rates.shape),
            in_hbm(),
        ],
        out_specs=tuple([in_vmem()] * 6),
        scratch_shapes=[
            pltpu.VMEM((40, groups), f32),
            pltpu.VMEM((2, BLOCK, width), bf16),
            pltpu.VMEM((TILES, 8 + ROWS, LANES), f32),
            pltpu.VMEM((TILES, 8 + ROWS, LANES), f32),
            pltpu.VMEM((BLOCK, LANES), i32),
            pltpu.SMEM((BLOCK // ROWS,), i32),
            pltpu.SemaphoreType.DMA((2,)),
        ],
        compiler_params=params(),
        name="front",
    )(place, *hbm(doc_lengths, short_taps, decay_rates, projected))


def edge_kernel(
    main_ref, head_ref, halo_ref, taps_ref, srel_ref, live_ref, tail_ref,
    product_out, contrib_out, edge_out, tapsq_out, srel_out, live_out,
    window_ref, product_ref, contrib_ref, sems, pass_sems,
):
    width = main_ref.shape[1]
    row = iota((BLOCK, LANES), 0)
    kept = jnp.where(row >= srel_ref[BLOCK - 1 : BLOCK], 1.0, 0.0).astype(bf16)
    rel = (row - srel_ref[...])[0:8]
    lane_group = iota((MODES, LANES), 1) // GROUP
    passed = [
        pltpu.make_async_copy(halo_ref.at[:, 0:width], edge_out, pass_sems.at[0]),
        pltpu.make_async_copy(taps_ref.at[0:8], tapsq_out, pass_sems.at[1]),
        pltpu.make_async_copy(srel_ref, srel_out, pass_sems.at[2]),
        pltpu.make_async_copy(live_ref, live_out, pass_sems.at[3]),
    ]
    for copy in passed:
        copy.start()

    def body(j, slot):
        values = []
        for p in range(2):
            past = halo_ref[:, tile(j + (1 + p) * (width // LANES))].astype(f32)
            window = window_ref.at[slot, p]
            window[0:8] = past
            window[8:16] = head_ref[p, :, tile(j)].astype(f32)
            line = 8 * (p + 1)
            summed = window[8:16] * taps_ref[line : line + 1, tile(j)]
            for offset in range(1, SHORT):
                term = window[8 - offset : 16 - offset]
                term = term * taps_ref[line + offset : line + offset + 1, tile(j)]
                summed = summed + jnp.where(rel >= offset, term, 0.0)
            values.append(summed)
        first = values[0] * values[1]
        rest = main_ref[0:16, tile(j)].astype(f32)[8:16]
        both = jnp.concatenate([first, rest], axis=0).astype(bf16)
        product = jnp.concatenate([both, main_ref[16:BLOCK, tile(j)]], axis=0)
        product_ref[:, tile(j)] = product
        all_modes = jnp.dot(
            tail_ref[tile(j), :], product * kept, preferred_element_type=f32
        )
        contrib = all_modes[0:MODES]
        for g in range(1, PER_TILE):
            contrib = jnp.where(
                lane_group == g, all_modes[g * MODES : (g + 1) * MODES], contrib
            )
        for p in range(PARTS):
            contrib_ref[p, j] = contrib[p * PART : (p + 1) * PART].astype(bf16)

    def copies(c):
        at = pl.ds(pl.multiple_of(c * WIDE, LANES), WIDE)
        tiles = pl.ds(pl.multiple_of(c * CHUNK, CHUNK), CHUNK)
        return (
            pltpu.make_async_copy(product_ref.at[:, at], product_out.at[:, at], sems.at[0, c]),
            pltpu.make_async_copy(contrib_ref.at[:, tiles], contrib_out.at[:, tiles], sems.at[1, c]),
        )

    def chunk(c, carry):
        def inner(i, more):
            for k in range(TILES):
                body(c * CHUNK + i * TILES + k, k)
            return more

        lax.fori_loop(0, CHUNK // TILES, inner, 0)
        for copy in copies(c):
            copy.start()
        return carry

    chunks = width // WIDE
    lax.fori_loop(0, chunks, chunk, 0)
    for copy in passed:
        copy.wait()
    for c in range(chunks):
        for copy in copies(c):
            copy.wait()


def make_edge(main, head, halo, tapsx, srel, live, tail):
    width = main.shape[1]
    shape = pltpu.HBM
    return pl.pallas_call(
        edge_kernel,
        out_shape=(
            shape((BLOCK, width), bf16),
            shape((PARTS, width // LANES, PART, LANES), bf16),
            shape((8, width), bf16),
            shape((8, width), f32),
            shape(srel.shape, i32),
            shape(live.shape, f32),
        ),
        in_specs=[in_vmem()] * 7,
        out_specs=tuple([in_hbm()] * 6),
        scratch_shapes=[
            pltpu.VMEM((TILES, 2, 16, LANES), f32),
            pltpu.VMEM((BLOCK, width), bf16),
            pltpu.VMEM((PARTS, width // LANES, PART, LANES), bf16),
            pltpu.SemaphoreType.DMA((2, width // WIDE)),
            pltpu.SemaphoreType.DMA((4,)),
        ],
        compiler_params=params(),
        name="edge",
    )(main, head, halo, tapsx, srel, live, tail)


def tables_kernel(
    srel_ref, rates_ref, scaled_ref, medium_ref,
    dec_ref, own_ref, med_ref, ratesx_ref,
    long_ref, lines_ref,
):
    row = iota((BLOCK, LANES), 0)
    lane = iota((BLOCK, LANES), 1)
    old = srel_ref[...] < 0
    own_mode = iota((MODES, LANES), 0) == iota((MODES, LANES), 1) % MODES
    ahead = (iota((8, LANES), 0) + 1).astype(f32)
    behind = (7 - iota((8, LANES), 0)).astype(f32)
    lines_ref[0:MODES] = rates_ref[...]
    lines_ref[MODES:] = scaled_ref[...]
    long_ref[...] = jnp.zeros(long_ref.shape, f32)
    ahead_of = lane - row // MODES

    def body(j, k, half):
        spread = expanded(lines_ref, j, half)
        ratesx_ref[:, tile(j)] = spread[0:MODES]
        rate = jnp.sum(jnp.where(own_mode, spread[0:MODES], 0.0), axis=0, keepdims=True)
        scale = jnp.sum(jnp.where(own_mode, spread[MODES:], 0.0), axis=0, keepdims=True)
        by_eight = jnp.exp(-8.0 * rate)
        decay = run_of(scale * jnp.exp(-rate * ahead), by_eight, False)
        dec_ref[:, tile(j)] = jnp.where(old, decay, 0.0).astype(bf16)
        power = run_of(scale * jnp.exp(-rate * behind), by_eight, True)
        upper = power.astype(bf16)
        lower = (power - upper.astype(f32)).astype(bf16)
        first = (j - half * (LANES // PER_TILE)) * PER_TILE
        hot = jnp.where(ahead_of == first, 1.0, 0.0).astype(bf16)
        long_ref[half] += jnp.dot(
            jnp.concatenate([upper, lower], axis=1),
            jnp.concatenate([hot, hot], axis=0),
            preferred_element_type=f32,
        )

    for_halves(medium_ref.shape[1], body)
    flip = jnp.where(row + lane == BLOCK - 1, 1.0, 0.0)
    for h in range(long_ref.shape[0]):
        medium = jnp.dot(
            flip, medium_ref[:, tile(h)], precision=HIGHEST, preferred_element_type=f32
        )
        med_ref[tile(h), :] = medium.T
        own_ref[tile(h), :] = (medium + long_ref[h]).T


def make_tables(srel, decay_rates, scaled, medium_taps, width):
    groups = medium_taps.shape[1]
    shape = jax.ShapeDtypeStruct
    return pl.pallas_call(
        tables_kernel,
        grid=(1,),
        out_shape=(
            pltpu.HBM((BLOCK, width), bf16),
            shape((groups, BLOCK), f32),
            pltpu.HBM((groups, BLOCK), f32),
            shape((MODES, width), f32),
        ),
        in_specs=[
            fixed((BLOCK, LANES)),
            fixed(decay_rates.shape),
            fixed(scaled.shape),
            fixed(medium_taps.shape),
        ],
        out_specs=tuple([in_vmem()] * 4),
        scratch_shapes=[
            pltpu.VMEM((groups // LANES, BLOCK, LANES), f32),
            pltpu.VMEM((2 * MODES, groups), f32),
        ],
        compiler_params=params(),
        name="tables",
    )(*hbm(srel, decay_rates, scaled, medium_taps))


def find_near(rel_ref, near_ref):
    for r in range(BLOCK // ROWS):
        least = jnp.min(rel_ref[r * ROWS : (r + 1) * ROWS].astype(f32))
        near_ref[r] = (least < SHORT - 1).astype(i32)


def by_rows(near_ref, work):
    for r in range(BLOCK // ROWS):
        near = near_ref[r] != 0
        pl.when(near)(lambda at=r * ROWS: work(at, True))
        pl.when(jnp.logical_not(near))(lambda at=r * ROWS: work(at, False))


def in_row_parts(rel_ref, near_ref, work):
    find_near(rel_ref, near_ref)
    by_rows(near_ref, work)


def feature_of(raw_ref, past, taps_ref, part, j, at, rel_ref, window_ref, masked):
    if at:
        past = raw_ref[at - 16 : at, tile(j)].astype(f32)[8:16]
    window_ref[0:8] = past
    window_ref[8 : 8 + ROWS] = raw_ref[at : at + ROWS, tile(j)].astype(f32)
    summed = window_ref[8 : 8 + ROWS] * taps_ref[8 * part : 8 * part + 1, tile(j)]
    for offset in range(1, SHORT):
        tap = taps_ref[8 * part + offset : 8 * part + offset + 1, tile(j)]
        term = window_ref[8 - offset : 8 - offset + ROWS] * tap
        if masked:
            term = jnp.where(rel_ref[at : at + ROWS] >= offset, term, 0.0)
        summed = summed + term
    return summed


HALF = BLOCK // 2


def set_masks(srel_ref, mask_ref, left_ref, right_ref, lower):
    row = iota((BLOCK, LANES), 0)
    lane = iota((BLOCK, LANES), 1)
    near = slice(0, HALF) if lower else slice(HALF, BLOCK)

    def within(rows, column):
        if lower:
            return (column <= row[rows]) & (column >= srel_ref[rows])
        return (column > row[rows]) & (column - BLOCK >= srel_ref[rows])

    every = slice(0, BLOCK)
    mask_ref[...] = jnp.where(within(every, lane), 1.0, 0.0).astype(bf16)
    side = lane[near]
    valid = within(near, side % HALF + (0 if lower else HALF))
    left_ref[...] = jnp.where(valid & (side < HALF), 1.0, 0.0).astype(bf16)
    right_ref[...] = jnp.where(valid & (side >= HALF), 1.0, 0.0).astype(bf16)


def mask_scratch():
    return [
        pltpu.VMEM((BLOCK, LANES), bf16),
        pltpu.VMEM((HALF, LANES), bf16),
        pltpu.VMEM((HALF, LANES), bf16),
    ]


def band_sum(j, x_ref, taps_ref, masks, lower):
    mask_ref, left_ref, right_ref = masks
    lane_group = iota((1, LANES), 1) // GROUP

    def only(values, count):
        return jnp.concatenate(
            [
                values * jnp.where(lane_group % count == i, 1.0, 0.0).astype(bf16)
                for i in range(count)
            ],
            axis=0,
        )

    x = x_ref[:, tile(j)]
    near = 0 if lower else HALF
    far = HALF - near
    both = only(x, 2)
    four = only(x[near : near + HALF], 4)
    taps = taps_ref[pl.ds(pl.multiple_of(j * PER_TILE, PER_TILE), PER_TILE), :]
    rings = []
    for g in range(PER_TILE):
        line = jnp.broadcast_to(taps[g : g + 1], (16, BLOCK))
        rings.append(pltpu.roll(line, 1, 1, stride=1, stride_axis=0).astype(bf16))

    def rows_from(g, first, shift):
        parts = []
        for k in range(HALF // 16):
            amount = (first + 16 * k + shift) % BLOCK
            parts.append(pltpu.roll(rings[g], amount, 1) if amount else rings[g])
        return jnp.concatenate(parts, axis=0)

    full_mask = mask_ref[far : far + HALF]
    pairs = [
        jnp.concatenate(
            [rows_from(2 * p + i, far, 0) * full_mask for i in range(2)], axis=1
        )
        for p in range(PER_TILE // 2)
    ]
    out = jnp.dot(jnp.concatenate(pairs, axis=0), both, preferred_element_type=f32)
    pair_of = iota((HALF, LANES), 1) // (2 * GROUP)
    full = out[0:HALF]
    for p in range(1, PER_TILE // 2):
        full = jnp.where(pair_of == p, out[p * HALF : (p + 1) * HALF], full)
    left_shift, right_shift = (0, HALF) if lower else (HALF, 0)
    quads = []
    for q in range(PER_TILE // 4):
        sides = []
        for g in (4 * q, 4 * q + 2):
            left = rows_from(g, near, left_shift) * left_ref[...]
            right = rows_from(g + 1, near, right_shift) * right_ref[...]
            sides.append(left + right)
        quads.append(jnp.concatenate(sides, axis=1))
    out = jnp.dot(jnp.concatenate(quads, axis=0), four, preferred_element_type=f32)
    partial = jnp.where(pair_of >= 2, out[HALF:], out[0:HALF])
    return jnp.concatenate([partial, full] if lower else [full, partial], axis=0)


def own_kernel(
    which_ref, srel_ref, x_ref, own_ref, skip_ref, rates_ref, live_ref,
    acc_ref, decay_ref, live_out,
    mask_ref, left_ref, right_ref,
):
    masks = (mask_ref, left_ref, right_ref)

    @pl.when(pl.program_id(0) == 0)
    def _():
        set_masks(srel_ref, *masks, True)
        decay_ref[...] = jnp.exp(-rates_ref[...] * float(BLOCK))
        live_out[...] = live_ref[...]

    def body(j, k):
        acc = skip_ref[:, tile(j)] * x_ref[:, tile(j)].astype(f32)
        acc_ref[:, tile(j)] = acc + band_sum(j, x_ref, own_ref, masks, True)

    for_tiles(CHUNK, body, CHUNK)


def cols(rows, first=0):
    return pl.BlockSpec((rows, WIDE), lambda j, *_: (0, first + j))


def whole(shape):
    return pl.BlockSpec(shape, lambda *_: (0,) * len(shape))


def make_own(which, srel, product, own, skip, ratesx, live):
    width = product.shape[1]
    tiles = width // LANES
    shape = jax.ShapeDtypeStruct
    return pl.pallas_call(
        own_kernel,
        out_shape=(
            pltpu.HBM((BLOCK, width), f32),
            shape((PART, LANES), f32),
            shape(live.shape, f32),
        ),
        grid_spec=pltpu.PrefetchScalarGridSpec(
            num_scalar_prefetch=1,
            grid=(width // WIDE,),
            in_specs=[
                whole((BLOCK, LANES)),
                cols(BLOCK),
                pl.BlockSpec((WIDE // GROUP, LANES), lambda j, *_: (j, 0)),
                cols(1),
                pl.BlockSpec((8, LANES), lambda _, at: (at[0] // tiles, at[0] % tiles)),
                whole(live.shape),
            ],
            out_specs=(cols(BLOCK), whole((PART, LANES)), whole(live.shape)),
            scratch_shapes=mask_scratch(),
        ),
        compiler_params=params(20),
        name="own",
    )(which, *hbm(srel, product), own, *hbm(skip), ratesx, *hbm(live))


def earlier_kernel(
    q_ref, hq_ref, tapsq_ref, x_ref, taps_ref, srel_ref, acc_ref, dec_ref,
    out_ref, dec_out, query_ref,
    mask_ref, left_ref, right_ref, wq_ref, rel_ref, near_ref,
):
    masks = (mask_ref, left_ref, right_ref)
    row = iota((BLOCK, LANES), 0)
    dec_out[...] = dec_ref[...]

    @pl.when(pl.program_id(0) == 0)
    def _():
        set_masks(srel_ref, *masks, False)
        rel_ref[...] = row - srel_ref[...]
        find_near(rel_ref, near_ref)

    def rows_of_query(at, masked):
        def ask(j, k):
            past = hq_ref[:, tile(j)].astype(f32)
            query_ref[at : at + ROWS, tile(j)] = feature_of(
                q_ref, past, tapsq_ref, 0, j, at, rel_ref, wq_ref.at[k], masked
            )

        for_tiles(CHUNK, ask, CHUNK)

    by_rows(near_ref, rows_of_query)

    def body(j, k):
        band = band_sum(j, x_ref, taps_ref, masks, False)
        out_ref[:, tile(j)] = acc_ref[:, tile(j)] + band

    for_tiles(CHUNK, body, CHUNK)


def make_earlier(projected, edge, tapsq, before, med, srel, acc, dec):
    width = acc.shape[1]
    shape = jax.ShapeDtypeStruct
    return pl.pallas_call(
        earlier_kernel,
        grid=(width // WIDE,),
        out_shape=(
            shape(acc.shape, f32),
            shape(acc.shape, bf16),
            pltpu.HBM(acc.shape, f32),
        ),
        in_specs=[
            columns(BLOCK),
            columns(8),
            columns(8),
            columns(BLOCK),
            rows_of(WIDE // GROUP),
            fixed((BLOCK, LANES)),
            columns(BLOCK),
            columns(BLOCK),
        ],
        out_specs=(columns(BLOCK), columns(BLOCK), columns(BLOCK)),
        scratch_shapes=mask_scratch()
        + [
            pltpu.VMEM((CHUNK, 8 + ROWS, LANES), f32),
            pltpu.VMEM((BLOCK, LANES), i32),
            pltpu.SMEM((BLOCK // ROWS,), i32),
        ],
        compiler_params=params(20),
        name="earlier",
    )(*hbm(projected, edge, tapsq, before, med, srel, acc, dec))


def totals_kernel(terms_ref, decay_ref, live_ref, out_ref):
    decay = decay_ref[...]
    state = jnp.zeros((PART, LANES), f32)
    kept = jnp.ones((PART, LANES), f32)
    for b in range(terms_ref.shape[0]):
        factor = live_ref[b : b + 1] * decay
        state = factor * state + terms_ref[b].astype(f32)
        kept = factor * kept
    out_ref[0] = state
    out_ref[1] = kept


def make_totals(terms, decay, live):
    return pl.pallas_call(
        totals_kernel,
        out_shape=jax.ShapeDtypeStruct((2, PART, LANES), f32),
        in_specs=[in_vmem()] * 3,
        out_specs=in_vmem(),
        compiler_params=params(),
        name="totals",
    )(terms, decay, live)


def states_kernel(terms_ref, decay_ref, live_ref, one_ref, two_ref, out_ref):
    decay = decay_ref[...]
    state = one_ref[0] + one_ref[1] * two_ref[0]
    for b in range(terms_ref.shape[0]):
        out_ref[b] = state.astype(bf16)
        state = live_ref[b : b + 1] * decay * state + terms_ref[b].astype(f32)


def make_states(terms, decay, live, one, two):
    return pl.pallas_call(
        states_kernel,
        out_shape=pltpu.HBM(terms.shape, bf16),
        in_specs=[in_vmem()] * 5,
        out_specs=in_vmem(),
        compiler_params=params(),
        name="states",
    )(terms, decay, live, one, two)


def final_kernel(
    acc_ref, query_hbm, dec_ref, state_ref, out_hbm,
    query_ref, filtered_ref, out_ref, sems,
):
    width = acc_ref.shape[1]
    chunks = width // WIDE

    def span(c):
        return pl.ds(pl.multiple_of(c * WIDE, LANES), WIDE)

    def fetch(c):
        return pltpu.make_async_copy(
            query_hbm.at[:, span(c)], query_ref.at[:, span(c)], sems.at[0, c]
        )

    def send(c):
        return pltpu.make_async_copy(
            out_ref.at[:, span(c)], out_hbm.at[:, span(c)], sems.at[1, c]
        )

    for c in range(chunks):
        fetch(c).start()
    same = iota((LANES, LANES), 0) // MODES == iota((LANES, LANES), 1) // GROUP
    keep = jnp.where(same, 1.0, 0.0).astype(bf16)

    def carry_in(j, k):
        one = jnp.concatenate([state_ref[p, j] for p in range(PARTS)], axis=0)
        spread = jnp.concatenate([one] * PER_TILE, axis=0) * keep
        carried = jnp.dot(dec_ref[:, tile(j)], spread, preferred_element_type=f32)
        filtered_ref[:, tile(j)] = (acc_ref[:, tile(j)] + carried).astype(bf16)

    for_tiles(width // LANES, carry_in)

    def chunk(c, carry):
        fetch(c).wait()

        def inner(j, k):
            at = tile(c * CHUNK + j)
            filtered = filtered_ref[:, at].astype(f32)
            out_ref[:, at] = (query_ref[:, at] * filtered).astype(bf16)

        for_tiles(CHUNK, inner)
        send(c).start()
        return carry

    lax.fori_loop(0, chunks, chunk, 0)
    for c in range(chunks):
        send(c).wait()


def make_final(acc, query, dec, state):
    chunks = acc.shape[1] // WIDE
    return pl.pallas_call(
        final_kernel,
        out_shape=pltpu.HBM(acc.shape, bf16),
        in_specs=[in_vmem(), in_hbm(), in_vmem(), in_vmem()],
        out_specs=in_hbm(),
        scratch_shapes=[
            pltpu.VMEM(acc.shape, f32),
            pltpu.VMEM(acc.shape, bf16),
            pltpu.VMEM(acc.shape, bf16),
            pltpu.SemaphoreType.DMA((2, chunks)),
        ],
        compiler_params=params(),
        name="final",
    )(acc, *hbm(query), dec, state)


def per_device(projected, doc_lengths, short_taps, medium_taps, decay_rates, residues, skip_gain):
    ts_count = lax.axis_size("ts")
    ctx_count = lax.axis_size("ctx")
    count = ts_count * ctx_count
    ctx = lax.axis_index("ctx")
    index = ctx * ts_count + lax.axis_index("ts")
    size = SPAN * ts_count
    which = (index % size).astype(i32)
    groups = [[s * size + j for j in range(size)] for s in range(count // size)]
    onward = [(i, i + 1) for i in range(count - 1)]
    width = projected.shape[1] // 3

    def from_ctx(value, by):
        return lax.ppermute(value, "ctx", [(i, i + by) for i in range(ctx_count - by)])

    halo = lax.ppermute(projected[BLOCK - 8 :], FLAT, onward)
    place = jnp.stack([index * BLOCK, (index - which) * BLOCK]).astype(i32)
    srel, live, tapsx, tail, main, head = make_front(
        place, doc_lengths, short_taps, decay_rates, projected, size
    )
    product, contrib, edge, tapsq, srel, live = make_edge(
        main, head, halo, tapsx, srel, live, tail
    )
    items = contrib.reshape(size, PART, LANES)
    terms = lax.all_to_all(
        items, FLAT, split_axis=0, concat_axis=0, tiled=True, axis_index_groups=groups
    )
    before = lax.ppermute(product, FLAT, onward)
    scaled = residues * jnp.sqrt(-jnp.expm1(-2.0 * decay_rates))
    dec, own, med, ratesx = make_tables(srel, decay_rates, scaled, medium_taps, width)
    acc, decay, near = make_own(
        which.reshape(1), srel, product, own, skip_gain.reshape(1, -1), ratesx, live
    )
    totals = make_totals(terms, decay, near)
    one = from_ctx(totals, SPAN)
    two = from_ctx(totals, 2 * SPAN)
    states = make_states(terms, decay, near, one, two)
    back = lax.all_to_all(
        states, FLAT, split_axis=0, concat_axis=0, tiled=True, axis_index_groups=groups
    )
    acc, dec, query = make_earlier(projected, edge, tapsq, before, med, srel, acc, dec)
    return make_final(acc, query, dec, back.reshape(PARTS, width // LANES, PART, LANES))


def solution(mesh):
    return jax.shard_map(
        per_device,
        mesh=mesh,
        in_specs=(P(FLAT, None), P(), P(), P(), P(), P(), P()),
        out_specs=P(FLAT, None),
        check_vma=False,
    )
```
